256 devices in a mesh: loop: 16 (over x, z_lo), rep: 16 (over z_hi, y, core).
Axes of the slice: x: 4, y: 4, z: 8 (z_hi: 2, z_lo: 4; z = z_hi * 4 + z_lo), core: 2. Of those that a mesh axis runs over, the one named last changes fastest.
Arguments:
- features: float32 [8192, 128], P('loop'), may hold values from -6 to 6
- weight: float32 [128, 256], replicated, may hold values from -0.5 to 0.5
- bias: float32 [256], replicated, may hold values from -3 to 3
- tile_values: float32 [4096, 128, 128], P(('loop', 'rep')), may hold values from -0.125 to 0.125
- tile_rows: int32 [4096], P(('loop', 'rep')), may hold values from 0 to 63, as said below
- tile_cols: int32 [4096], P(('loop', 'rep')), may hold values from 0 to 63, as said below
- tile_count: int32 [256], P(('loop', 'rep')), may hold values from 1 to 16, as said below
- cotangent: float32 [8192, 256], P('loop'), may hold values from -0.6 to 0.6
Outputs:
- output: float32 [8192, 256], P('loop')
- grad_features: float32 [8192, 128], P('loop')
- grad_weight: float32 [128, 256], replicated
- grad_bias: float32 [256], replicated
The draws below stay inside these ranges and needn't reach their ends.
Inputs may be any that keep to these rules, and one draw needn't show every extreme that they name: `tile_rows`: every slot of a device at loop index l names a row block from l * 4 to (l + 1) * 4 - 1. `tile_cols`: for every loop index m, the live slots of one device name at most 2 different column blocks from m * 4 to (m + 1) * 4 - 1; for every loop index some device names exactly 2 of one such range. `tile_count`: for every loop index some device has all 16 slots live.
All inputs are finite; a program needn't handle non-finite values.
Results may differ from the reference program's by a relative error of at most 0.0001.
Values sent between devices are 32-bit elements; how exact they have to be, the bound alone decides.
A program may use at most 64 MiB of HBM per device.

```python
import jax
import jax.numpy as jnp
from jax import lax

F_IN = 128
F_OUT = 256
TILE = 128
COL_CAP = 2
BLK_DEV = 4
TILE_DEV = 16
NODES = 8192
TILES = 4096
N_LOOP = 16
N_REP = 16


def tile_layout(key):
    devices = N_LOOP * N_REP
    keys = jax.random.split(jax.random.fold_in(key, 7), 8)
    slot_ids = jnp.arange(TILE_DEV, dtype=jnp.int32)[None, :]
    target_loop = jax.random.randint(keys[0], (devices, TILE_DEV), 0, N_LOOP)
    first_target = jax.random.randint(keys[1], (devices,), 0, N_LOOP)
    target_loop = jnp.where(slot_ids < COL_CAP, first_target[:, None], target_loop)
    which = jax.random.randint(keys[2], (devices, TILE_DEV), 0, COL_CAP)
    which = jnp.where(slot_ids < COL_CAP, slot_ids, which)
    scores = jax.random.randint(keys[3], (devices, N_LOOP, BLK_DEV), 0, 4096) * BLK_DEV
    scores = scores + jnp.arange(BLK_DEV, dtype=jnp.int32)
    column_sets = jnp.argsort(scores, axis=2, stable=True)[:, :, :COL_CAP].astype(jnp.int32)
    flat_sets = column_sets.reshape(devices, N_LOOP * COL_CAP)
    local_col = jnp.take_along_axis(flat_sets, target_loop * COL_CAP + which, axis=1)
    col_ids = target_loop * BLK_DEV + local_col
    device_loop = jnp.arange(devices, dtype=jnp.int32) // N_REP
    favoured = jax.random.randint(keys[4], (N_LOOP,), 0, BLK_DEV)[device_loop]
    row_draw = jax.random.randint(keys[5], (devices, TILE_DEV), 0, 2 * BLK_DEV)
    local_row = jnp.where(row_draw < BLK_DEV, row_draw, favoured[:, None])
    row_ids = device_loop[:, None] * BLK_DEV + local_row
    counts = jax.random.randint(keys[6], (N_LOOP, N_REP), 1, TILE_DEV + 1)
    full_rep = jax.random.randint(keys[7], (N_LOOP,), 0, N_REP)
    counts = jnp.where(jnp.arange(N_REP)[None, :] == full_rep[:, None], TILE_DEV, counts)
    return (row_ids.reshape(-1).astype(jnp.int32), col_ids.reshape(-1).astype(jnp.int32), counts.reshape(-1).astype(jnp.int32))


def draw_tile_rows(key, part):
    return tile_layout(key)[0]


def draw_tile_cols(key, part):
    return tile_layout(key)[1]


def draw_tile_count(key, part):
    return tile_layout(key)[2]


def block_scale(stream_key, shape, cuts, smallest, top_value):
    loudness, own = 1.0, jax.random.fold_in(stream_key, 6)
    for axis_at, shards_of in cuts:
        heights = jnp.exp(jax.random.uniform(jax.random.fold_in(own, axis_at), (shards_of,), jnp.float32, smallest / len(cuts), top_value / len(cuts)))
        loudness = loudness * jnp.repeat(heights, shape[axis_at] // shards_of).reshape([-1 if axis == axis_at else 1 for axis in range(len(shape))])
    return loudness


def gaussian(rng, extent, deviation, most, cuts=(), kind=jnp.bfloat16):
    factor_of = block_scale(rng, extent, cuts, -0.22, 0.18) if cuts else 1.0
    drawn = jax.random.normal(rng, extent, jnp.float32) * deviation * factor_of
    return jnp.minimum(jnp.maximum(drawn, -most), most).astype(kind)


def setup_inputs(seed: int = 0) -> dict:
    key_of = jax.random.split(jax.random.key(seed), 9)
    features = gaussian(key_of[0], (NODES, F_IN), 1.0, 6.0, ((0, 16),), jnp.float32)
    weight = gaussian(key_of[1], (F_IN, F_OUT), F_IN ** -0.5, 0.5, (), jnp.float32)
    bias = gaussian(key_of[2], (F_OUT,), 0.5, 3.0, (), jnp.float32)
    tile_values = gaussian(key_of[3], (TILES, TILE, TILE), (TILE * 16) ** -0.5, 0.125, ((0, 256),), jnp.float32)
    tile_rows = draw_tile_rows(jax.random.fold_in(key_of[8], 71), 0)
    tile_cols = draw_tile_cols(jax.random.fold_in(key_of[8], 71), 0)
    tile_count = draw_tile_count(jax.random.fold_in(key_of[8], 71), 0)
    cotangent = gaussian(key_of[7], (NODES, F_OUT), 0.1, 0.6, ((0, 16),), jnp.float32)
    return dict(features=features, weight=weight, bias=bias, tile_values=tile_values, tile_rows=tile_rows, tile_cols=tile_cols, tile_count=tile_count, cotangent=cotangent)


def block_product(tile_values, tile_rows, tile_cols, tile_count, dense_in, transpose):
    tile_side = tile_values.shape[1]
    nblocks = dense_in.shape[0] // tile_side
    width = dense_in.shape[1]
    blocks = dense_in.reshape(nblocks, tile_side, width)
    devices = tile_count.shape[0]
    values = tile_values.reshape(devices, -1, tile_side, tile_side)
    row_ids = tile_rows.reshape(devices, -1).astype(jnp.int32)
    col_ids = tile_cols.reshape(devices, -1).astype(jnp.int32)
    slot_ids = jnp.arange(values.shape[1], dtype=jnp.int32)
    live_slot = (slot_ids[None, :] < tile_count[:, None].astype(jnp.int32)).astype(jnp.float32)

    def step(running, portion):
        vals, rows_here, cols_here, alive = portion
        if transpose:
            source, target, pattern = rows_here, cols_here, "kji,kjf->kif"
        else:
            source, target, pattern = cols_here, rows_here, "kij,kjf->kif"
        product = jnp.einsum(pattern, vals, blocks[source], precision=lax.Precision.HIGHEST)
        product = product * alive[:, None, None]
        return running.at[target].add(product), None

    initial = jnp.zeros((nblocks, tile_side, width), jnp.float32)
    summed, _ = lax.scan(step, initial, (values, row_ids, col_ids, live_slot))
    return summed.reshape(nblocks * tile_side, width)


def reference(features, weight, bias, tile_values, tile_rows, tile_cols, tile_count, cotangent):
    aggregated = block_product(tile_values, tile_rows, tile_cols, tile_count, features, False)
    preactive = jnp.dot(aggregated, weight, precision=lax.Precision.HIGHEST) + bias
    logistic = jax.nn.sigmoid(preactive)
    output = preactive * logistic
    gradient = cotangent * logistic * (1.0 + preactive * (1.0 - logistic))
    grad_weight = jnp.dot(aggregated.T, gradient, precision=lax.Precision.HIGHEST)
    grad_bias = jnp.sum(gradient, axis=0)
    spread = jnp.dot(gradient, weight.T, precision=lax.Precision.HIGHEST)
    grad_features = block_product(tile_values, tile_rows, tile_cols, tile_count, spread, True)
    return output, grad_features, grad_weight, grad_bias
```

```python
import jax
import jax.numpy as jnp
from jax import lax
from jax.experimental import pallas as pl
from jax.experimental.pallas import tpu as pltpu
from jax.sharding import PartitionSpec as P

F32, BF16 = jnp.float32, jnp.bfloat16
ROWS_LAST = (((1,), (0,)), ((), ()))
BOTH_LAST = (((1,), (1,)), ((), ()))


def split(v):
    high = v.astype(BF16)
    return high, (v - high.astype(F32)).astype(BF16)


def dot3(a, b, dims=ROWS_LAST):
    def one(p, q):
        return lax.dot_general(p, q, dims, preferred_element_type=F32)

    return one(a[0], b[0]) + (one(a[0], b[1]) + one(a[1], b[0]))


def kernel(
    table_smem, table_any, features, weight, bias, tiles, cotangent,
    out, grad_features, grad_weight, grad_bias,
    sib_table, table_in, feat, tile, t_hi, t_lo, tt_hi, tt_lo,
    agg_part, y_in2, z_out2, z_in2, agg, out_stage, grad, s_hi, s_lo, chain,
    b1, b1_in, b2, b2_in, a1, a1_in, a2, a2_in, line, fin,
    gw, w_out, x_in5, z_out5, z_in5, y_in4, z_out4, z_in4, pay,
    local_sem, send_sem, recv_sem,
):
    loop, rep = lax.axis_index("loop"), lax.axis_index("rep")
    x, zl = lax.div(loop, 4), lax.rem(loop, 4)
    zh, y, c = lax.div(rep, 8), lax.rem(lax.div(rep, 2), 4), lax.rem(rep, 2)
    z = zh * 4 + zl

    def device(xx, yy, zz, cc):
        return {
            "loop": xx * 4 + lax.rem(zz, 4),
            "rep": lax.div(zz, 4) * 8 + yy * 2 + cc,
        }

    def at_x(d):
        return device(lax.rem(x + d + 4, 4), y, z, c)

    def at_y(d):
        return device(x, lax.rem(y + d + 4, 4), z, c)

    def at_z(d):
        return device(x, y, lax.rem(z + d + 8, 8), c)

    def along_a(d):
        return device(
            lax.rem(x + (1 - c) * d + 4, 4), y, lax.rem(z + c * d + 8, 8), c
        )

    def along_b(d):
        return device(
            lax.rem(x + c * d + 4, 4), y, lax.rem(z + (1 - c) * d + 8, 8), c
        )

    sibling = device(x, y, z, 1 - c)
    a, b = (1 - c) * x + c * zl, c * x + (1 - c) * zl

    def chunk(da, db):
        aa, bb = lax.rem(a + da + 4, 4), lax.rem(b + db + 4, 4)
        return c * 32 + (aa * (4 - 3 * c) + bb * (1 + 3 * c)) * 2

    counter = [0]
    sent = []

    def push(src, dst, to, recv=None):
        n = counter[0]
        counter[0] += 1
        copy = pltpu.make_async_remote_copy(
            src_ref=src,
            dst_ref=dst,
            send_sem=send_sem.at[n],
            recv_sem=recv_sem.at[n if recv is None else recv],
            device_id=to,
            device_id_type=pl.DeviceIdType.MESH,
        )
        copy.start()
        sent.append(copy)
        return copy

    own = [
        pltpu.make_async_copy(
            features.at[pl.ds(2 * h, 2)],
            feat.at[pl.ds(32 * h + 2 * loop, 2)],
            local_sem.at[h],
        )
        for h in range(2)
    ]
    for copy in own:
        copy.start()
    tiles_in = pltpu.make_async_copy(tiles, tile.at[pl.ds(0, 16)], local_sem.at[2])
    tiles_in.start()

    partners = [at_x(1), at_x(2), at_x(3), at_y(1), at_y(2), at_y(3)]
    partners += [at_z(1), at_z(2), at_z(4), at_z(6), at_z(7), sibling]
    barrier = pltpu.get_barrier_semaphore()
    for partner in partners:
        pl.semaphore_signal(
            barrier, inc=1, device_id=partner, device_id_type=pl.DeviceIdType.MESH
        )
    pl.semaphore_wait(barrier, len(partners))

    for copy in own:
        copy.wait()

    def block_pair(da, db):
        return feat.at[pl.ds(chunk(da, db), 2)]

    def one_block(da, db, j):
        return feat.at[pl.ds(chunk(da, db) + j, 1)]

    sib_chunks = 90

    def to_sibling(da, db):
        push(block_pair(da, db), block_pair(da, db), sibling, recv=sib_chunks)

    a_right = push(block_pair(0, 0), block_pair(0, 0), along_a(1))
    a_left = push(block_pair(0, 0), block_pair(0, 0), along_a(-1))
    b_right, b_left, b_fwd = {}, {}, {}

    def out_b(da):
        b_right[da] = push(block_pair(da, 0), block_pair(da, 0), along_b(1))
        b_left[da] = push(block_pair(da, 0), block_pair(da, 0), along_b(-1))

    def relay_b(da):
        b_right[da].wait_recv()
        first = push(one_block(da, -1, 0), one_block(da, -1, 0), along_b(1))
        to_sibling(da, -1)
        b_left[da].wait_recv()
        second = push(one_block(da, 1, 1), one_block(da, 1, 1), along_b(-1))
        to_sibling(da, 1)
        b_fwd[da] = (first, second)

    out_b(0)
    table_move = push(table_any, table_in, sibling)
    tiles_move = push(tiles, tile.at[pl.ds(16, 16)], sibling)

    tiles_in.wait()

    def split_tile(s):
        t_hi[s], t_lo[s] = split(tile[s])
        tt_hi[s], tt_lo[s] = split(tile[s].T)

    def split_tiles(start):
        def two(s, _):
            split_tile(start + 2 * s)
            split_tile(start + 2 * s + 1)
            return 0

        lax.fori_loop(0, 8, two, 0)

    a_right.wait_recv()
    a_fwd_right = push(one_block(-1, 0, 0), one_block(-1, 0, 0), along_a(1))
    out_b(-1)
    to_sibling(-1, 0)
    a_left.wait_recv()
    a_fwd_left = push(one_block(1, 0, 1), one_block(1, 0, 1), along_a(-1))
    out_b(1)
    to_sibling(1, 0)
    split_tiles(0)
    relay_b(0)
    a_fwd_right.wait_recv()
    a_fwd_left.wait_recv()
    out_b(2)
    to_sibling(2, 0)
    table_move.wait_recv()
    table_local = pltpu.make_async_copy(table_in, sib_table, local_sem.at[3])
    table_local.start()
    tiles_move.wait_recv()
    split_tiles(16)
    table_local.wait()
    for da in (-1, 1, 2):
        relay_b(da)
    for da in (0, -1, 1, 2):
        b_fwd[da][0].wait_recv()
        b_fwd[da][1].wait_recv()
        to_sibling(da, 2)
    pltpu.make_async_copy(
        feat.at[pl.ds(0, 30)], feat.at[pl.ds(0, 30)], recv_sem.at[sib_chunks]
    ).wait()

    agg_part[...] = jnp.zeros_like(agg_part)
    for side, table in enumerate((table_smem, sib_table)):

        def add_products(step, _, side=side, table=table):
            for u in range(4):
                s = step * 4 + u
                block = split(feat[table[0, s]])
                product = dot3((t_hi[16 * side + s], t_lo[16 * side + s]), block)
                row = table[0, 16 + s]
                for j in range(2):
                    keep = (row == 2 * c + j).astype(F32)
                    agg_part[128 * j : 128 * j + 128, :] += product * keep
            return 0

        lax.fori_loop(0, 4, add_products, 0)

    def reduce_rep(part, y_in, z_out, z_in):
        moves = []
        for d in (2, 1, 3):
            there = lax.rem(y + d, 4)
            moves.append(
                push(part.at[pl.ds(there * 64, 64)], y_in.at[y], at_y(d))
            )
        y_in[y] = part[pl.ds(pl.multiple_of(y * 64, 64), 64), :]
        for move in moves:
            move.wait_recv()
        z_out[...] = (y_in[0] + y_in[1]) + (y_in[2] + y_in[3])
        swap = push(z_out, z_in, at_z(4))
        swap.wait_recv()
        return z_out[...] + z_in[...]

    def gather_rep(buf, sem, whole):
        mine = buf.at[c * 4 + y]
        moves = [(d, push(mine, mine, at_y(d))) for d in (2, 1, 3)]
        push(mine, mine, sibling, recv=sem)
        for d, move in (moves[1], moves[2], moves[0]):
            move.wait_recv()
            got = buf.at[c * 4 + lax.rem(y - d + 4, 4)]
            push(got, got, sibling, recv=sem)
        pltpu.make_async_copy(
            buf.at[pl.ds(0, 4)], buf.at[pl.ds(0, 4)], recv_sem.at[sem]
        ).wait()

    total = reduce_rep(agg_part, y_in2, z_out2, z_in2)
    agg[c * 4 + y] = total
    gather_rep(agg, 91, None)

    weights = split(weight[...])
    for r in range(4):
        rows = slice(128 * r, 128 * r + 128)
        mine = agg[2 * r : 2 * r + 2].reshape(128, 128)
        pre = dot3(split(mine), weights) + bias[...]
        logistic = 1.0 / (1.0 + jnp.exp(-pre))
        out_stage[rows, :] = pre * logistic
        g = cotangent[rows, :] * logistic * (1.0 + pre * (1.0 - logistic))
        grad[rows, :] = g
        s_hi[r], s_lo[r] = split(dot3(split(g), weights, BOTH_LAST))
    out_move = pltpu.make_async_copy(out_stage, out, local_sem.at[4])
    out_move.start()

    chain[16] = jnp.zeros((128, 128), F32)
    chain[33] = jnp.zeros((128, 128), F32)
    for side, table in enumerate((table_smem, sib_table)):

        def add_transposed(step, _, side=side, table=table):
            for u in range(4):
                s = step * 4 + u
                row = table[0, 32 + s]
                product = dot3(
                    (tt_hi[16 * side + s], tt_lo[16 * side + s]),
                    (s_hi[row], s_lo[row]),
                )
                chain[17 * side + s] = product + chain[17 * side + table[0, 48 + s]]
            return 0

        lax.fori_loop(0, 4, add_transposed, 0)

    def dense(da, db, j):
        f = chunk(da, db) + j
        return chain[table_smem[0, 64 + f]] + chain[17 + sib_table[0, 64 + f]]

    order = (2, -1, 1, 0)
    to1 = {}
    for k, da in enumerate(order):
        b1[0, k] = dense(da, 2, 0)
        b1[1, k] = dense(da, 2, 1)
        to1[k] = (
            push(b1.at[0, k], b1_in.at[0, k], along_b(1)),
            push(b1.at[1, k], b1_in.at[1, k], along_b(-1)),
        )

    gw[...] = dot3(
        split(agg[...].reshape(512, 128).T), split(grad[...])
    )
    w_out[0:16, :] = gw[pl.ds(pl.multiple_of((c * 4 + y) * 16, 16), 16), :]
    w_out[16:24, :] = jnp.broadcast_to(
        jnp.sum(grad[...], axis=0, keepdims=True), (8, 256)
    )
    x_in5[x] = w_out[...]

    to2 = {}
    for k, da in enumerate(order):
        for i, d in ((0, 1), (1, -1)):
            b2[i, k, 1 - i] = dense(da, d, 1 - i)
            to1[k][i].wait_recv()
            b2[i, k, i] = dense(da, d, i) + b1_in[i, k]
            to2[k, i] = push(b2.at[i, k], b2_in.at[i, k], along_b(d))
    x_moves = [push(w_out, x_in5.at[x], at_x(d)) for d in (2, 1, 3)]
    for move in x_moves:
        move.wait_recv()
    z_out5[...] = (x_in5[0] + x_in5[1]) + (x_in5[2] + x_in5[3])
    z_in5[zl] = z_out5[...]
    z_moves = [push(z_out5, z_in5.at[zl], at_z(d)) for d in (2, 1, -1)]

    to3, to4 = {}, {}
    for k, da in enumerate(order):
        for j in range(2):
            line[k, j] = dense(da, 0, j)
        for i in range(2):
            to2[k, i].wait_recv()
        for j in range(2):
            line[k, j] += b2_in[0, k, j] + b2_in[1, k, j]
        if da == 2:
            to3 = (
                push(line.at[k, 0], a1_in.at[0], along_a(1)),
                push(line.at[k, 1], a1_in.at[1], along_a(-1)),
            )
        elif da != 0:
            i = 0 if da == 1 else 1
            to3[i].wait_recv()
            line[k, i] += a1_in[i]
            to4[i] = push(line.at[k], a2_in.at[i], along_a(da))
        else:
            to4[0].wait_recv()
            to4[1].wait_recv()
            for j in range(2):
                fin[128 * j : 128 * j + 128, :] = line[k, j] + (
                    a2_in[0, j] + a2_in[1, j]
                )
    for move in z_moves:
        move.wait_recv()
    total = reduce_rep(fin, y_in4, z_out4, z_in4)
    here = c * 4 + y
    pay[here, 0:64, :] = total
    summed = (z_in5[0] + z_in5[1]) + (z_in5[2] + z_in5[3])
    pay[here, 64:80, :] = summed[0:16, 0:128]
    pay[here, 80:96, :] = summed[0:16, 128:256]
    grad_bias[...] = summed[16:24, :]
    gather_rep(pay, 92, None)
    for i in range(8):
        grad_features[64 * i : 64 * i + 64, :] = pay[i, 0:64, :]
        grad_weight[16 * i : 16 * i + 16, 0:128] = pay[i, 64:80, :]
        grad_weight[16 * i : 16 * i + 16, 128:256] = pay[i, 80:96, :]
    out_move.wait()
    for copy in sent:
        copy.wait_send()


def make_table(tile_rows, tile_cols, tile_count):
    slots = tile_cols.shape[0]
    ids = jnp.arange(slots, dtype=jnp.int32)
    live = ids < tile_count[0]
    spot = lax.rem(lax.div(tile_cols, 2), 2) * 32 + lax.div(tile_cols, 4) * 2
    spot = spot + lax.rem(tile_cols, 2)
    row = lax.rem(tile_rows, 4)
    earlier = (spot[None, :] == spot[:, None]) & live[None, :]
    earlier = earlier & (ids[None, :] < ids[:, None])
    before = jnp.max(jnp.where(earlier, ids[None, :], -1), axis=1)
    blocks = jnp.arange(64, dtype=jnp.int32)
    match = (spot[None, :] == blocks[:, None]) & live[None, :]
    last = jnp.max(jnp.where(match, ids[None, :], -1), axis=1)
    none = slots
    return jnp.concatenate(
        [
            spot,
            jnp.where(live, row, -1),
            row,
            jnp.where(before < 0, none, before),
            jnp.where(last < 0, none, last),
        ]
    )[None, :]


def per_device(features, weight, bias, tile_values, tile_rows, tile_cols, tile_count, cotangent):
    table = make_table(tile_rows, tile_cols, tile_count)
    vmem, anywhere = pltpu.VMEM, pl.BlockSpec(memory_space=pl.ANY)
    in_vmem = pl.BlockSpec(memory_space=pltpu.VMEM)
    square = (128, 128)
    outs = pl.pallas_call(
        kernel,
        out_shape=(
            jax.ShapeDtypeStruct((512, 256), F32),
            jax.ShapeDtypeStruct((512, 128), F32),
            jax.ShapeDtypeStruct((128, 256), F32),
            jax.ShapeDtypeStruct((8, 256), F32),
        ),
        in_specs=[
            pl.BlockSpec(memory_space=pltpu.SMEM),
            anywhere,
            anywhere,
            in_vmem,
            in_vmem,
            anywhere,
            in_vmem,
        ],
        out_specs=(anywhere, in_vmem, in_vmem, in_vmem),
        scratch_shapes=[
            pltpu.SMEM((1, 128), jnp.int32),
            vmem((1, 128), jnp.int32),
            vmem((64, *square), F32),
            vmem((32, *square), F32),
            vmem((32, *square), BF16),
            vmem((32, *square), BF16),
            vmem((32, *square), BF16),
            vmem((32, *square), BF16),
            vmem((256, 128), F32),
            vmem((4, 64, 128), F32),
            vmem((64, 128), F32),
            vmem((64, 128), F32),
            vmem((8, 64, 128), F32),
            vmem((512, 256), F32),
            vmem((512, 256), F32),
            vmem((4, *square), BF16),
            vmem((4, *square), BF16),
            vmem((34, *square), F32),
            vmem((2, 4, *square), F32),
            vmem((2, 4, *square), F32),
            vmem((2, 4, 2, *square), F32),
            vmem((2, 4, 2, *square), F32),
            vmem((8, 128), F32),
            vmem((2, *square), F32),
            vmem((8, 128), F32),
            vmem((2, 2, *square), F32),
            vmem((4, 2, *square), F32),
            vmem((256, 128), F32),
            vmem((128, 256), F32),
            vmem((24, 256), F32),
            vmem((4, 24, 256), F32),
            vmem((24, 256), F32),
            vmem((4, 24, 256), F32),
            vmem((4, 64, 128), F32),
            vmem((64, 128), F32),
            vmem((64, 128), F32),
            vmem((8, 96, 128), F32),
            pltpu.SemaphoreType.DMA((5,)),
            pltpu.SemaphoreType.DMA((96,)),
            pltpu.SemaphoreType.DMA((96,)),
        ],
        compiler_params=pltpu.CompilerParams(
            collective_id=0, has_side_effects=True, vmem_limit_bytes=40 * 1024 * 1024
        ),
        cost_estimate=pl.CostEstimate(
            flops=400_000_000, bytes_accessed=4_000_000, transcendentals=131072
        ),
    )(
        table,
        table,
        features.reshape(4, *square),
        weight,
        bias[None, :],
        tile_values,
        cotangent,
    )
    output, grad_features, grad_weight, grad_bias = outs
    return output, grad_features, grad_weight, grad_bias[0]


def solution(mesh):
    return jax.shard_map(
        per_device,
        mesh=mesh,
        in_specs=(
            P("loop", None),
            P(),
            P(),
            P(("loop", "rep"), None, None),
            P(("loop", "rep")),
            P(("loop", "rep")),
            P(("loop", "rep")),
            P("loop", None),
        ),
        out_specs=(P("loop", None), P("loop", None), P(), P()),
        check_vma=False,
    )
```

```python
import jax
import jax.numpy as jnp
from jax import lax
from jax.experimental import pallas as pl
from jax.experimental.pallas import tpu as pltpu
from jax.sharding import PartitionSpec as P

F32, BF16 = jnp.float32, jnp.bfloat16


def split(v):
    high = v.astype(BF16)
    return high, (v - high.astype(F32)).astype(BF16)


def left(v):
    high, low = split(v)
    return jnp.concatenate([high, high, low], axis=1)


def right(v):
    high, low = split(v)
    return jnp.concatenate([high, low, high], axis=0)


def dot(a, b):
    return lax.dot_general(a, b, (((1,), (0,)), ((), ())), preferred_element_type=F32)


def kernel(
    tile_rows, tile_cols, tile_count, features, weight_in, bias_in, tiles, cotangent_in,
    out, grad_features, grad_weight, grad_bias,
    table_out, table_in, own_table, sib_table, feat, tile, weight, bias, cotangent,
    t_left, tt_left, w_right, wt_right,
    agg_part, y_in2, z_out2, z_in2, agg, out_stage, grad, s_right, chain,
    b_out, b_far, b_in, b_far_in, a_in, a_far_in, line, fin,
    gw, w_out, x_in5, z_out5, z_in5, y_in4, z_out4, z_in4, pay,
    local_sem, send_sem, recv_sem,
):
    loop, rep = lax.axis_index("loop"), lax.axis_index("rep")
    x, zl = lax.div(loop, 4), lax.rem(loop, 4)
    zh, y, c = lax.div(rep, 8), lax.rem(lax.div(rep, 2), 4), lax.rem(rep, 2)
    z = zh * 4 + zl

    def device(xx, yy, zz, cc):
        return {
            "loop": xx * 4 + lax.rem(zz, 4),
            "rep": lax.div(zz, 4) * 8 + yy * 2 + cc,
        }

    def at_x(d):
        return device(lax.rem(x + d + 4, 4), y, z, c)

    def at_y(d):
        return device(x, lax.rem(y + d + 4, 4), z, c)

    def at_z(d):
        return device(x, y, lax.rem(z + d + 8, 8), c)

    def along_a(d):
        return device(
            lax.rem(x + (1 - c) * d + 4, 4), y, lax.rem(z + c * d + 8, 8), c
        )

    def along_b(d):
        return device(
            lax.rem(x + c * d + 4, 4), y, lax.rem(z + (1 - c) * d + 8, 8), c
        )

    sibling = device(x, y, z, 1 - c)
    a, b = (1 - c) * x + c * zl, c * x + (1 - c) * zl

    def chunk(da, db):
        aa, bb = lax.rem(a + da + 4, 4), lax.rem(b + db + 4, 4)
        return c * 32 + (aa * (4 - 3 * c) + bb * (1 + 3 * c)) * 2

    counter = [0]
    sent = []

    def push(src, dst, to, recv=None):
        n = counter[0]
        counter[0] += 1
        copy = pltpu.make_async_remote_copy(
            src_ref=src,
            dst_ref=dst,
            send_sem=send_sem.at[n],
            recv_sem=recv_sem.at[n if recv is None else recv],
            device_id=to,
            device_id_type=pl.DeviceIdType.MESH,
        )
        copy.start()
        sent.append(copy)
        return copy

    own = [
        pltpu.make_async_copy(
            features.at[pl.ds(2 * h, 2)],
            feat.at[pl.ds(32 * h + 2 * loop, 2)],
            local_sem.at[h],
        )
        for h in range(2)
    ]
    for copy in own:
        copy.start()
    tiles_in = pltpu.make_async_copy(tiles, tile.at[pl.ds(0, 16)], local_sem.at[2])
    tiles_in.start()
    layer_in = [
        pltpu.make_async_copy(src, dst, local_sem.at[5 + n])
        for n, (src, dst) in enumerate(
            ((weight_in, weight), (bias_in, bias), (cotangent_in, cotangent))
        )
    ]
    for copy in layer_in:
        copy.start()

    partners = [at_x(1), at_x(2), at_x(3), at_y(1), at_y(2), at_y(3)]
    partners += [at_z(1), at_z(2), at_z(6), at_z(7), sibling]
    barrier = pltpu.get_barrier_semaphore()
    for partner in partners:
        pl.semaphore_signal(
            barrier, inc=1, device_id=partner, device_id_type=pl.DeviceIdType.MESH
        )

    table_out[...] = make_table(tile_rows, tile_cols, tile_count)
    table_local = pltpu.make_async_copy(table_out, own_table, local_sem.at[8])
    table_local.start()
    for copy in own:
        copy.wait()
    pl.semaphore_wait(barrier, len(partners))

    def block_pair(da, db):
        return feat.at[pl.ds(chunk(da, db), 2)]

    def one_block(da, db, j):
        return feat.at[pl.ds(chunk(da, db) + j, 1)]

    sib_chunks = 90

    def to_sibling(da, db):
        push(block_pair(da, db), block_pair(da, db), sibling, recv=sib_chunks)

    relayed = (0, -1, 1)
    a_near = [push(block_pair(0, 0), block_pair(0, 0), along_a(d)) for d in (1, -1)]
    b_near, b_two = {}, {}

    def far(src, along):
        return [push(src.at[pl.ds(j, 1)], src.at[pl.ds(j, 1)], along(4 * j - 2)) for j in range(2)]

    def out_b(da):
        b_near[da] = [
            push(block_pair(da, 0), block_pair(da, 0), along_b(d)) for d in (1, -1)
        ]
        if da not in relayed:
            b_two[da] = far(block_pair(da, 0), along_b)

    def near_b(da):
        for i, d in ((0, 1), (1, -1)):
            b_near[da][i].wait_recv()
            if da in relayed:
                view = one_block(da, -d, i)
                b_two.setdefault(da, []).append(push(view, view, along_b(d)))
            to_sibling(da, -d)

    out_b(0)
    a_far = far(block_pair(0, 0), along_a)
    table_move = push(table_out, table_in, sibling)
    tiles_move = push(tiles, tile.at[pl.ds(16, 16)], sibling)

    def split_tiles(start):
        def two(n, _):
            for s in (start + 2 * n, start + 2 * n + 1):
                t_left[s] = left(tile[s])
                tt_left[s] = left(tile[s].T)
            return 0

        lax.fori_loop(0, 8, two, 0)

    for i, d in ((0, 1), (1, -1)):
        a_near[i].wait_recv()
        out_b(-d)
    to_sibling(-1, 0)
    to_sibling(1, 0)
    for move in a_far:
        move.wait_recv()
    out_b(2)
    to_sibling(2, 0)
    near_b(0)
    table_local.wait()
    table_move.wait_recv()
    table_local = pltpu.make_async_copy(table_in, sib_table, local_sem.at[3])
    table_local.start()
    tiles_in.wait()
    split_tiles(0)
    near_b(-1)
    near_b(1)
    tiles_move.wait_recv()
    split_tiles(16)
    for copy in layer_in:
        copy.wait()
    w_right[...] = right(weight[...])
    wt_right[...] = right(weight[...].T)
    table_local.wait()
    near_b(2)
    for da in (0, -1, 1, 2):
        for j in range(2):
            b_two[da][j].wait_recv()
            view = one_block(da, 2, j)
            push(view, view, sibling, recv=sib_chunks)
    pltpu.make_async_copy(
        feat.at[pl.ds(0, 30)], feat.at[pl.ds(0, 30)], recv_sem.at[sib_chunks]
    ).wait()

    agg_part[...] = jnp.zeros_like(agg_part)
    for side, table in enumerate((own_table, sib_table)):

        def add_products(step, _, side=side, table=table):
            for u in range(4):
                s = step * 4 + u
                product = dot(t_left[16 * side + s], right(feat[table[0, s]]))
                row = table[0, 16 + s]
                for j in range(2):
                    keep = (row == 2 * c + j).astype(F32)
                    agg_part[128 * j : 128 * j + 128, :] += product * keep
            return 0

        lax.fori_loop(0, 4, add_products, 0)

    def reduce_rep(part, y_in, z_out, z_in):
        moves = []
        for d in (2, 1, 3):
            there = lax.rem(y + d, 4)
            moves.append(
                push(part.at[pl.ds(there * 64, 64)], y_in.at[y], at_y(d))
            )
        y_in[y] = part[pl.ds(pl.multiple_of(y * 64, 64), 64), :]
        for move in moves:
            move.wait_recv()
        z_out[...] = (y_in[0] + y_in[1]) + (y_in[2] + y_in[3])
        swap = push(z_out, z_in, at_z(4))
        swap.wait_recv()
        return z_out[...] + z_in[...]

    def gather_rep(buf, sem):
        mine = buf.at[c * 4 + y]
        moves = [(d, push(mine, mine, at_y(d))) for d in (2, 1, 3)]
        push(mine, mine, sibling, recv=sem)
        for d, move in (moves[1], moves[2], moves[0]):
            move.wait_recv()
            got = buf.at[c * 4 + lax.rem(y - d + 4, 4)]
            push(got, got, sibling, recv=sem)
        pltpu.make_async_copy(
            buf.at[pl.ds(0, 4)], buf.at[pl.ds(0, 4)], recv_sem.at[sem]
        ).wait()

    total = reduce_rep(agg_part, y_in2, z_out2, z_in2)
    agg[c * 4 + y] = total
    gather_rep(agg, 91)

    for r in range(4):
        rows = slice(128 * r, 128 * r + 128)
        mine = agg[2 * r : 2 * r + 2].reshape(128, 128)
        pre = dot(left(mine), w_right[...]) + bias[...]
        logistic = 1.0 / (1.0 + jnp.exp(-pre))
        out_stage[rows, :] = pre * logistic
        g = cotangent[rows, :] * logistic * (1.0 + pre * (1.0 - logistic))
        grad[rows, :] = g
        s_right[r] = right(dot(left(g), wt_right[...]))
    out_move = pltpu.make_async_copy(out_stage, out, local_sem.at[4])
    out_move.start()

    chain[16] = jnp.zeros((128, 128), F32)
    chain[33] = jnp.zeros((128, 128), F32)
    for side, table in enumerate((own_table, sib_table)):

        def add_transposed(step, _, side=side, table=table):
            for u in range(4):
                s = step * 4 + u
                row = table[0, 32 + s]
                product = dot(tt_left[16 * side + s], s_right[row])
                chain[17 * side + s] = product + chain[17 * side + table[0, 48 + s]]
            return 0

        lax.fori_loop(0, 4, add_transposed, 0)


    def dense(da, db, j):
        f = chunk(da, db) + j
        return chain[own_table[0, 64 + f]] + chain[17 + sib_table[0, 64 + f]]

    order = (2, -1, 1, 0)
    summed_on_way = (2, -1, 1)
    to_near, to_far = {}, {}
    for k, da in enumerate(order):
        for j in range(2):
            b_far[k, j] = dense(da, 2, j)
            step = 1 - 2 * j if da in summed_on_way else 4 * j - 2
            to_far[k, j] = push(b_far.at[k, j], b_far_in.at[k, j], along_b(step))

    def to_next(k, da):
        for i, d in ((0, 1), (1, -1)):
            b_out[i, k, 1 - i] = dense(da, d, 1 - i)
            b_out[i, k, i] = dense(da, d, i)
            if da in summed_on_way:
                to_far[k, i].wait_recv()
                b_out[i, k, i] += b_far_in[k, i]
            to_near[k, i] = push(b_out.at[i, k], b_in.at[i, k], along_b(d))

    to_next(3, 0)

    gw[...] = dot(left(agg[...].reshape(512, 128).T), right(grad[...]))
    w_out[0:16, :] = gw[pl.ds(pl.multiple_of((c * 4 + y) * 16, 16), 16), :]
    w_out[16:24, :] = jnp.broadcast_to(
        jnp.sum(grad[...], axis=0, keepdims=True), (8, 256)
    )
    x_in5[x] = w_out[...]
    for k, da in enumerate(order[:3]):
        to_next(k, da)
    x_moves = [push(w_out, x_in5.at[x], at_x(d)) for d in (2, 1, 3)]
    for k, da in enumerate(order):
        for j in range(2):
            line[k, j] = dense(da, 0, j)
    for move in x_moves:
        move.wait_recv()
    z_out5[...] = (x_in5[0] + x_in5[1]) + (x_in5[2] + x_in5[3])
    z_in5[zl] = z_out5[...]
    z_moves = [push(z_out5, z_in5.at[zl], at_z(d)) for d in (2, 1, -1)]

    to_a, to_a_far = {}, []
    for k, da in enumerate(order):
        for i in range(2):
            to_near[k, i].wait_recv()
            if da not in summed_on_way:
                to_far[k, i].wait_recv()
        for j in range(2):
            line[k, j] += b_in[0, k, j] + b_in[1, k, j]
            if da not in summed_on_way:
                line[k, j] += b_far_in[k, j]
        if da == 2:
            to_a_far = [
                push(line.at[k, j], a_far_in.at[j], along_a(4 * j - 2)) for j in range(2)
            ]
        elif da != 0:
            i = 0 if da == 1 else 1
            to_a[i] = push(line.at[k], a_in.at[i], along_a(da))
    for move in (*to_a_far, to_a[0], to_a[1]):
        move.wait_recv()
    for j in range(2):
        fin[128 * j : 128 * j + 128, :] = (line[3, j] + a_far_in[j]) + (
            a_in[0, j] + a_in[1, j]
        )
    for move in z_moves:
        move.wait_recv()
    total = reduce_rep(fin, y_in4, z_out4, z_in4)
    here = c * 4 + y
    pay[here, 0:64, :] = total
    summed = (z_in5[0] + z_in5[1]) + (z_in5[2] + z_in5[3])
    pay[here, 64:80, :] = summed[0:16, 0:128]
    pay[here, 80:96, :] = summed[0:16, 128:256]
    grad_bias[...] = summed[16:17, :]
    gather_rep(pay, 92)
    for i in range(8):
        grad_features[64 * i : 64 * i + 64, :] = pay[i, 0:64, :]
        grad_weight[16 * i : 16 * i + 16, 0:128] = pay[i, 64:80, :]
        grad_weight[16 * i : 16 * i + 16, 128:256] = pay[i, 80:96, :]
    out_move.wait()
    for copy in sent:
        copy.wait_send()


def make_table(tile_rows, tile_cols, tile_count):
    lane = lax.broadcasted_iota(jnp.int32, (1, 128), 1)
    slot, part = lax.rem(lane, 16), lax.div(lane, 16)
    spots = []
    for s in range(16):
        col = tile_cols[s]
        spots.append(
            lax.rem(lax.div(col, 2), 2) * 32 + lax.div(col, 4) * 2 + lax.rem(col, 2)
        )
    spot = jnp.zeros((1, 128), jnp.int32)
    row = jnp.zeros((1, 128), jnp.int32)
    for s in range(16):
        spot = jnp.where(slot == s, spots[s], spot)
        row = jnp.where(slot == s, lax.rem(tile_rows[s], 4), row)
    live = slot < tile_count[0]
    spot_here = jnp.where(part >= 4, lane - 64, spot)
    limit = jnp.where(part >= 4, 16, slot)
    found = jnp.full((1, 128), 16, jnp.int32)
    for s in range(16):
        hit = (spot_here == spots[s]) & (limit > s) & (tile_count[0] > s)
        found = jnp.where(hit, s, found)
    table = jnp.where(part == 0, spot, found)
    table = jnp.where(part == 1, jnp.where(live, row, -1), table)
    return jnp.where(part == 2, row, table)


def finish_kernel(*refs):
    sems = refs[8]
    moves = [pltpu.make_async_copy(refs[n], refs[4 + n], sems.at[n]) for n in range(4)]
    for move in moves:
        move.start()
    for move in moves:
        move.wait()


def per_device(features, weight, bias, tile_values, tile_rows, tile_cols, tile_count, cotangent):
    vmem, hbm = pltpu.VMEM, pl.BlockSpec(memory_space=pltpu.HBM)
    smem = pl.BlockSpec(memory_space=pltpu.SMEM)
    anywhere = pl.BlockSpec(memory_space=pl.ANY)
    in_vmem = pl.BlockSpec(memory_space=pltpu.VMEM)
    square = (128, 128)
    shapes = (
        jax.ShapeDtypeStruct((512, 256), F32),
        jax.ShapeDtypeStruct((512, 128), F32),
        jax.ShapeDtypeStruct((128, 256), F32),
        jax.ShapeDtypeStruct((1, 256), F32),
    )
    outs = pl.pallas_call(
        kernel,
        out_shape=shapes,
        in_specs=[smem, smem, smem, hbm, hbm, hbm, hbm, hbm],
        out_specs=(hbm, in_vmem, in_vmem, in_vmem),
        scratch_shapes=[
            vmem((1, 128), jnp.int32),
            vmem((1, 128), jnp.int32),
            pltpu.SMEM((1, 128), jnp.int32),
            pltpu.SMEM((1, 128), jnp.int32),
            vmem((64, *square), F32),
            vmem((32, *square), F32),
            vmem((128, 256), F32),
            vmem((1, 256), F32),
            vmem((512, 256), F32),
            vmem((32, 128, 384), BF16),
            vmem((32, 128, 384), BF16),
            vmem((384, 256), BF16),
            vmem((768, 128), BF16),
            vmem((256, 128), F32),
            vmem((4, 64, 128), F32),
            vmem((64, 128), F32),
            vmem((64, 128), F32),
            vmem((8, 64, 128), F32),
            vmem((512, 256), F32),
            vmem((512, 256), F32),
            vmem((4, 384, 128), BF16),
            vmem((34, *square), F32),
            vmem((2, 4, 2, *square), F32),
            vmem((4, 2, *square), F32),
            vmem((2, 4, 2, *square), F32),
            vmem((4, 2, *square), F32),
            vmem((2, 2, *square), F32),
            vmem((2, *square), F32),
            vmem((4, 2, *square), F32),
            vmem((256, 128), F32),
            vmem((128, 256), F32),
            vmem((24, 256), F32),
            vmem((4, 24, 256), F32),
            vmem((24, 256), F32),
            vmem((4, 24, 256), F32),
            vmem((4, 64, 128), F32),
            vmem((64, 128), F32),
            vmem((64, 128), F32),
            vmem((8, 96, 128), F32),
            pltpu.SemaphoreType.DMA((9,)),
            pltpu.SemaphoreType.DMA((96,)),
            pltpu.SemaphoreType.DMA((96,)),
        ],
        compiler_params=pltpu.CompilerParams(
            collective_id=0, has_side_effects=True, vmem_limit_bytes=60 * 1024 * 1024
        ),
        cost_estimate=pl.CostEstimate(
            flops=400_000_000, bytes_accessed=4_000_000, transcendentals=131072
        ),
    )(
        tile_rows,
        tile_cols,
        tile_count,
        features.reshape(4, *square),
        weight,
        bias[None, :],
        tile_values,
        cotangent,
    )
    output, grad_features, grad_weight, grad_bias = pl.pallas_call(
        finish_kernel,
        out_shape=shapes,
        in_specs=[in_vmem] * 4,
        out_specs=[hbm] * 4,
        scratch_shapes=[pltpu.SemaphoreType.DMA((4,))],
    )(*outs)
    return output, grad_features, grad_weight, grad_bias[0]


def solution(mesh):
    return jax.shard_map(
        per_device,
        mesh=mesh,
        in_specs=(
            P("loop", None),
            P(),
            P(),
            P(("loop", "rep"), None, None),
            P(("loop", "rep")),
            P(("loop", "rep")),
            P(("loop", "rep")),
            P("loop", None),
        ),
        out_specs=(P("loop", None), P("loop", None), P(), P()),
        check_vma=False,
    )
```

```python
import jax
import jax.numpy as jnp
from jax import lax
from jax.experimental import pallas as pl
from jax.experimental.pallas import tpu as pltpu
from jax.sharding import PartitionSpec as P

F32, BF16 = jnp.float32, jnp.bfloat16


def split(v):
    high = v.astype(BF16)
    return high, (v - high.astype(F32)).astype(BF16)


def left(v):
    high, low = split(v)
    return jnp.concatenate([high, high, low], axis=1)


def right(v):
    high, low = split(v)
    return jnp.concatenate([high, low, high], axis=0)


def dot(a, b):
    return lax.dot_general(a, b, (((1,), (0,)), ((), ())), preferred_element_type=F32)


def kernel(
    tile_rows, tile_cols, tile_count, features, weight_in, bias_in, tiles, cotangent_in,
    out, grad_features, grad_weight, grad_bias,
    table_out, table_in, own_table, sib_table, feat, tile, weight, bias, cotangent,
    t_left, tt_left, w_right, wt_right,
    agg_part, core_in, half, y_in2, z_out2, z_in2, agg, out_stage, grad, s_right, chain,
    b_out, b_far, b_in, b_far_in, line, p_in, y_out, y_in4, y_sum, line_in,
    gw, w_out, x_in5, z_out5, z_in5, z_out4, z_in4, pay,
    local_sem, send_sem, recv_sem,
):
    loop, rep = lax.axis_index("loop"), lax.axis_index("rep")
    x, zl = lax.div(loop, 4), lax.rem(loop, 4)
    zh, y, c = lax.div(rep, 8), lax.rem(lax.div(rep, 2), 4), lax.rem(rep, 2)
    z = zh * 4 + zl

    def device(xx, yy, zz, cc):
        return {
            "loop": xx * 4 + lax.rem(zz, 4),
            "rep": lax.div(zz, 4) * 8 + yy * 2 + cc,
        }

    def at_x(d):
        return device(lax.rem(x + d + 4, 4), y, z, c)

    def at_y(d):
        return device(x, lax.rem(y + d + 4, 4), z, c)

    def at_z(d):
        return device(x, y, lax.rem(z + d + 8, 8), c)

    def along_a(d, dy=0):
        return device(
            lax.rem(x + (1 - c) * d + 4, 4),
            lax.rem(y + dy, 4),
            lax.rem(z + c * d + 8, 8),
            c,
        )

    def along_b(d):
        return device(
            lax.rem(x + c * d + 4, 4), y, lax.rem(z + (1 - c) * d + 8, 8), c
        )

    sibling = device(x, y, z, 1 - c)
    a, b = (1 - c) * x + c * zl, c * x + (1 - c) * zl

    def chunk(da, db):
        aa, bb = lax.rem(a + da + 4, 4), lax.rem(b + db + 4, 4)
        return (aa * (4 - 3 * c) + bb * (1 + 3 * c)) * 2

    counter = [0]
    sent = []

    def push(src, dst, to, recv=None):
        n = counter[0]
        counter[0] += 1
        copy = pltpu.make_async_remote_copy(
            src_ref=src,
            dst_ref=dst,
            send_sem=send_sem.at[n],
            recv_sem=recv_sem.at[n if recv is None else recv],
            device_id=to,
            device_id_type=pl.DeviceIdType.MESH,
        )
        copy.start()
        sent.append(copy)
        return copy

    own = pltpu.make_async_copy(
        features.at[pl.ds(4 * c, 4)], feat.at[pl.ds(4 * loop, 4)], local_sem.at[0]
    )
    own.start()
    tiles_in = pltpu.make_async_copy(tiles, tile.at[pl.ds(0, 16)], local_sem.at[2])
    tiles_in.start()
    layer_in = [
        pltpu.make_async_copy(src, dst, local_sem.at[5 + n])
        for n, (src, dst) in enumerate(
            ((weight_in, weight), (bias_in, bias), (cotangent_in, cotangent))
        )
    ]
    for copy in layer_in:
        copy.start()

    partners = [at_x(1), at_x(2), at_x(3), at_y(1), at_y(2), at_y(3)]
    partners += [at_z(1), at_z(2), at_z(6), at_z(7), sibling]
    barrier = pltpu.get_barrier_semaphore()
    for partner in partners:
        pl.semaphore_signal(
            barrier, inc=1, device_id=partner, device_id_type=pl.DeviceIdType.MESH
        )

    table_out[...] = make_table(tile_rows, tile_cols, tile_count)
    table_local = pltpu.make_async_copy(table_out, own_table, local_sem.at[8])
    table_local.start()
    own.wait()
    pl.semaphore_wait(barrier, len(partners))

    def rows_of(da, db, first=0, pieces=4):
        return feat.at[pl.ds(2 * chunk(da, db) + first, pieces)]

    by_pieces = (0,)
    a_near = [push(rows_of(0, 0), rows_of(0, 0), along_a(d)) for d in (1, -1)]
    b_near, b_two, y_spread = {}, {}, []
    two_away = 4 * lax.div(y, 2) - 2

    def far(da, along):
        views = [rows_of(da, 0, 2 * j, 2) for j in range(2)]
        return [push(views[j], views[j], along(4 * j - 2)) for j in range(2)]

    def out_b(da):
        view = rows_of(da, 0, y, 1) if da in by_pieces else rows_of(da, 0)
        b_near[da] = [push(view, view, along_b(d)) for d in (1, -1)]
        if da in by_pieces:
            b_two[da] = [push(view, view, along_b(two_away))]
        elif da == 2:
            b_two[da] = far(da, along_b)

    def near_b(da):
        for i, d in ((0, 1), (1, -1)):
            b_near[da][i].wait_recv()
            if da in by_pieces:
                spread(da, -d)
            elif da != 2:
                view = rows_of(da, -d, 2 * i, 2)
                b_two.setdefault(da, []).append(push(view, view, along_b(d)))
        if da in by_pieces:
            b_two[da][0].wait_recv()
            spread(da, 2)

    def spread(da, db):
        view = rows_of(da, db, y, 1)
        y_spread.extend(push(view, view, at_y(d)) for d in (2, 1, 3))

    out_b(0)
    a_far = far(0, along_a)
    table_move = push(table_out, table_in, sibling)
    tiles_move = push(tiles, tile.at[pl.ds(16, 16)], sibling)

    def split_tiles(start):
        def two(n, _):
            for s in (start + 2 * n, start + 2 * n + 1):
                t_left[s] = left(tile[s])
                tt_left[s] = left(tile[s].T)
            return 0

        lax.fori_loop(0, 8, two, 0)

    near_b(0)
    for i, d in ((0, 1), (1, -1)):
        a_near[i].wait_recv()
        out_b(-d)
    for move in a_far:
        move.wait_recv()
    out_b(2)
    table_local.wait()
    table_move.wait_recv()
    table_local = pltpu.make_async_copy(table_in, sib_table, local_sem.at[3])
    table_local.start()
    tiles_in.wait()
    split_tiles(0)
    near_b(-1)
    near_b(1)
    tiles_move.wait_recv()
    split_tiles(16)
    for copy in layer_in:
        copy.wait()
    chain[16] = jnp.zeros((128, 128), F32)
    chain[33] = jnp.zeros((128, 128), F32)
    w_right[...] = right(weight[...])
    wt_right[...] = right(weight[...].T)
    table_local.wait()
    near_b(2)
    for da in (-1, 1, 2):
        if da not in by_pieces:
            for move in b_two[da]:
                move.wait_recv()
    for move in y_spread:
        move.wait_recv()

    for side, table in enumerate((own_table, sib_table)):

        def add_products(step, _, side=side, table=table):
            for u in range(4):
                s = step * 4 + u
                spot = 2 * lax.rem(table[0, s], 32)
                block = right(feat[pl.ds(spot, 2)].reshape(128, 128))
                product = dot(t_left[16 * side + s], block)
                chain[17 * side + s] = product + chain[17 * side + table[0, 16 + s]]
            return 0

        lax.fori_loop(0, 4, add_products, 0)
    for j in range(4):
        f = 4 * c + j
        agg_part[j] = chain[own_table[1, f]] + chain[17 + sib_table[1, f]]

    other = push(agg_part.at[pl.ds(2 * (1 - c), 2)], core_in, sibling)
    other.wait_recv()
    for j in range(2):
        half[128 * j : 128 * j + 128, :] = agg_part[2 * c + j] + core_in[j]

    def sum_z(value, z_out, z_in):
        z_out[...] = value
        swap = push(z_out, z_in, at_z(4))
        swap.wait_recv()
        return z_out[...] + z_in[...]

    def reduce_rep(part, y_in, z_out, z_in):
        moves = []
        for d in (2, 1, 3):
            there = lax.rem(y + d, 4)
            moves.append(
                push(part.at[pl.ds(there * 64, 64)], y_in.at[y], at_y(d))
            )
        y_in[y] = part[pl.ds(pl.multiple_of(y * 64, 64), 64), :]
        for move in moves:
            move.wait_recv()
        return sum_z((y_in[0] + y_in[1]) + (y_in[2] + y_in[3]), z_out, z_in)

    def gather_rep(buf, sem):
        mine = buf.at[c * 4 + y]
        moves = [(d, push(mine, mine, at_y(d))) for d in (2, 1, 3)]
        push(mine, mine, sibling, recv=sem)
        for d, move in (moves[1], moves[2], moves[0]):
            move.wait_recv()
            got = buf.at[c * 4 + lax.rem(y - d + 4, 4)]
            push(got, got, sibling, recv=sem)
        pltpu.make_async_copy(
            buf.at[pl.ds(0, 4)], buf.at[pl.ds(0, 4)], recv_sem.at[sem]
        ).wait()

    total = reduce_rep(half, y_in2, z_out2, z_in2)
    agg[c * 4 + y] = total
    gather_rep(agg, 111)

    for r in range(4):
        rows = slice(128 * r, 128 * r + 128)
        mine = agg[2 * r : 2 * r + 2].reshape(128, 128)
        pre = dot(left(mine), w_right[...]) + bias[...]
        logistic = 1.0 / (1.0 + jnp.exp(-pre))
        out_stage[rows, :] = pre * logistic
        g = cotangent[rows, :] * logistic * (1.0 + pre * (1.0 - logistic))
        grad[rows, :] = g
        s_right[r] = right(dot(left(g), wt_right[...]))
    out_move = pltpu.make_async_copy(out_stage, out, local_sem.at[4])
    out_move.start()

    for side, table in enumerate((own_table, sib_table)):

        def add_transposed(step, _, side=side, table=table):
            for u in range(4):
                s = step * 4 + u
                row = table[0, 32 + s]
                product = dot(tt_left[16 * side + s], s_right[row])
                chain[17 * side + s] = product + chain[17 * side + table[0, 48 + s]]
            return 0

        lax.fori_loop(0, 4, add_transposed, 0)


    def dense(da, db, j):
        f = 64 + 32 * c + chunk(da, db) + j
        return chain[own_table[0, f]] + chain[17 + sib_table[0, f]]

    order = (2, -1, 1, 0)
    to_near, to_far = {}, {}
    for k, da in enumerate(order[:3]):
        for j in range(2):
            b_far[k, j] = dense(da, 2, j)
            to_far[k, j] = push(b_far.at[k, j], b_far_in.at[k, j], along_b(1 - 2 * j))

    y_moves = []
    for n, db in enumerate((2, -1, 1, 0)):
        for j in range(2):
            y_out[n, 2 * j : 2 * j + 2] = dense(0, db, j).reshape(2, 64, 128)
        for dy in (2, 1, 3):
            piece = lax.rem(y + dy, 4)
            y_moves.append(push(y_out.at[n, piece], y_in4.at[n, dy - 1], at_y(dy)))

    def to_next(k, da):
        for i, d in ((0, 1), (1, -1)):
            b_out[i, k, 1 - i] = dense(da, d, 1 - i)
            to_far[k, i].wait_recv()
            b_out[i, k, i] = dense(da, d, i) + b_far_in[k, i]
            to_near[k, i] = push(b_out.at[i, k], b_in.at[i, k], along_b(d))

    gw[...] = dot(left(agg[...].reshape(512, 128).T), right(grad[...]))
    w_out[0:16, :] = gw[pl.ds(pl.multiple_of((c * 4 + y) * 16, 16), 16), :]
    w_out[16:24, :] = jnp.broadcast_to(
        jnp.sum(grad[...], axis=0, keepdims=True), (8, 256)
    )
    x_in5[x] = w_out[...]
    x_moves = [push(w_out, x_in5.at[x], at_x(d)) for d in (2, 1, 3)]
    for k, da in enumerate(order[:3]):
        to_next(k, da)
    for move in y_moves:
        move.wait_recv()
    line_moves = []
    for n, d in enumerate((two_away, -1, 1, 0)):
        y_sum[n] = (y_out[n, y] + y_in4[n, 0]) + (y_in4[n, 1] + y_in4[n, 2])
        if n < 3:
            line_moves.append(push(y_sum.at[n], line_in.at[n], along_b(d)))

    pieces = []
    for k, da in enumerate(order[:3]):
        for i in range(2):
            to_near[k, i].wait_recv()
        for j in range(2):
            value = dense(da, 0, j) + (b_in[0, k, j] + b_in[1, k, j])
            line[k, 2 * j : 2 * j + 2] = value.reshape(2, 64, 128)
        for dy in (2, 1, 3, 0):
            piece = lax.rem(y + dy, 4)
            d = 4 * lax.div(piece, 2) - 2 if da == 2 else da
            pieces.append(push(line.at[k, piece], p_in.at[k, dy], along_a(d, dy)))
    for move in x_moves:
        move.wait_recv()
    z_out5[...] = (x_in5[0] + x_in5[1]) + (x_in5[2] + x_in5[3])
    z_in5[zl] = z_out5[...]
    z_moves = [push(z_out5, z_in5.at[zl], at_z(d)) for d in (2, 1, -1)]
    total = y_sum[3]
    for n in range(3):
        line_moves[n].wait_recv()
        total += line_in[n]
    for k in range(3):
        for n, dy in enumerate((2, 1, 3, 0)):
            pieces[4 * k + n].wait_recv()
            total += p_in[k, dy]
    total = sum_z(total, z_out4, z_in4)
    for move in z_moves:
        move.wait_recv()
    here = c * 4 + y
    pay[here, 0:64, :] = total
    summed = (z_in5[0] + z_in5[1]) + (z_in5[2] + z_in5[3])
    pay[here, 64:80, :] = summed[0:16, 0:128]
    pay[here, 80:96, :] = summed[0:16, 128:256]
    grad_bias[...] = summed[16:17, :]
    gather_rep(pay, 112)
    for i in range(8):
        grad_features[64 * i : 64 * i + 64, :] = pay[i, 0:64, :]
        grad_weight[16 * i : 16 * i + 16, 0:128] = pay[i, 64:80, :]
        grad_weight[16 * i : 16 * i + 16, 128:256] = pay[i, 80:96, :]
    out_move.wait()
    for copy in sent:
        copy.wait_send()


def make_table(tile_rows, tile_cols, tile_count):
    lane = lax.broadcasted_iota(jnp.int32, (1, 128), 1)
    slot, part = lax.rem(lane, 16), lax.div(lane, 16)
    spots, lines = [], []
    for s in range(16):
        col = tile_cols[s]
        side = lax.rem(lax.div(col, 2), 2)
        spots.append(side * 32 + lax.div(col, 4) * 2 + lax.rem(col, 2))
        lines.append(side * 4 + lax.rem(tile_rows[s], 4))
    spot = jnp.zeros((1, 128), jnp.int32)
    line = jnp.zeros((1, 128), jnp.int32)
    for s in range(16):
        spot = jnp.where(slot == s, spots[s], spot)
        line = jnp.where(slot == s, lines[s], line)
    by_spot = jnp.where(part >= 4, lane - 64, spot)
    limit = jnp.where(part >= 4, 16, slot)
    found = jnp.full((1, 128), 16, jnp.int32)
    found_line, last_line = found, found
    for s in range(16):
        live = tile_count[0] > s
        found = jnp.where((by_spot == spots[s]) & (limit > s) & live, s, found)
        found_line = jnp.where((line == lines[s]) & (slot > s) & live, s, found_line)
        last_line = jnp.where((lane == lines[s]) & live, s, last_line)
    table = jnp.where(part == 0, spot, found)
    table = jnp.where(part == 1, found_line, table)
    table = jnp.where(part == 2, lax.rem(line, 4), table)
    return jnp.concatenate([table, last_line], axis=0)


def finish_kernel(*refs):
    sems = refs[8]
    moves = [pltpu.make_async_copy(refs[n], refs[4 + n], sems.at[n]) for n in range(4)]
    for move in moves:
        move.start()
    for move in moves:
        move.wait()


def per_device(features, weight, bias, tile_values, tile_rows, tile_cols, tile_count, cotangent):
    vmem, hbm = pltpu.VMEM, pl.BlockSpec(memory_space=pltpu.HBM)
    smem = pl.BlockSpec(memory_space=pltpu.SMEM)
    anywhere = pl.BlockSpec(memory_space=pl.ANY)
    in_vmem = pl.BlockSpec(memory_space=pltpu.VMEM)
    square = (128, 128)
    shapes = (
        jax.ShapeDtypeStruct((512, 256), F32),
        jax.ShapeDtypeStruct((512, 128), F32),
        jax.ShapeDtypeStruct((128, 256), F32),
        jax.ShapeDtypeStruct((1, 256), F32),
    )
    outs = pl.pallas_call(
        kernel,
        out_shape=shapes,
        in_specs=[smem, smem, smem, hbm, hbm, hbm, hbm, hbm],
        out_specs=(hbm, in_vmem, in_vmem, in_vmem),
        scratch_shapes=[
            vmem((2, 128), jnp.int32),
            vmem((2, 128), jnp.int32),
            pltpu.SMEM((2, 128), jnp.int32),
            pltpu.SMEM((2, 128), jnp.int32),
            vmem((64, 64, 128), F32),
            vmem((32, *square), F32),
            vmem((128, 256), F32),
            vmem((1, 256), F32),
            vmem((512, 256), F32),
            vmem((32, 128, 384), BF16),
            vmem((32, 128, 384), BF16),
            vmem((384, 256), BF16),
            vmem((768, 128), BF16),
            vmem((4, *square), F32),
            vmem((2, *square), F32),
            vmem((256, 128), F32),
            vmem((4, 64, 128), F32),
            vmem((64, 128), F32),
            vmem((64, 128), F32),
            vmem((8, 64, 128), F32),
            vmem((512, 256), F32),
            vmem((512, 256), F32),
            vmem((4, 384, 128), BF16),
            vmem((34, *square), F32),
            vmem((2, 4, 2, *square), F32),
            vmem((4, 2, *square), F32),
            vmem((2, 4, 2, *square), F32),
            vmem((4, 2, *square), F32),
            vmem((3, 4, 64, 128), F32),
            vmem((3, 4, 64, 128), F32),
            vmem((4, 4, 64, 128), F32),
            vmem((4, 3, 64, 128), F32),
            vmem((4, 64, 128), F32),
            vmem((3, 64, 128), F32),
            vmem((128, 256), F32),
            vmem((24, 256), F32),
            vmem((4, 24, 256), F32),
            vmem((24, 256), F32),
            vmem((4, 24, 256), F32),
            vmem((64, 128), F32),
            vmem((64, 128), F32),
            vmem((8, 96, 128), F32),
            pltpu.SemaphoreType.DMA((9,)),
            pltpu.SemaphoreType.DMA((120,)),
            pltpu.SemaphoreType.DMA((120,)),
        ],
        compiler_params=pltpu.CompilerParams(
            collective_id=0, has_side_effects=True, vmem_limit_bytes=60 * 1024 * 1024
        ),
        cost_estimate=pl.CostEstimate(
            flops=400_000_000, bytes_accessed=4_000_000, transcendentals=131072
        ),
    )(
        tile_rows,
        tile_cols,
        tile_count,
        features.reshape(8, 64, 128),
        weight,
        bias[None, :],
        tile_values,
        cotangent,
    )
    output, grad_features, grad_weight, grad_bias = pl.pallas_call(
        finish_kernel,
        out_shape=shapes,
        in_specs=[in_vmem] * 4,
        out_specs=[hbm] * 4,
        scratch_shapes=[pltpu.SemaphoreType.DMA((4,))],
    )(*outs)
    return output, grad_features, grad_weight, grad_bias[0]


def solution(mesh):
    return jax.shard_map(
        per_device,
        mesh=mesh,
        in_specs=(
            P("loop", None),
            P(),
            P(),
            P(("loop", "rep"), None, None),
            P(("loop", "rep")),
            P(("loop", "rep")),
            P(("loop", "rep")),
            P("loop", None),
        ),
        out_specs=(P("loop", None), P("loop", None), P(), P()),
        check_vma=False,
    )
```

```python
import jax
import jax.numpy as jnp
from jax import lax
from jax.experimental import pallas as pl
from jax.experimental.pallas import tpu as pltpu
from jax.sharding import PartitionSpec as P

F32, BF16 = jnp.float32, jnp.bfloat16


def split(v):
    high = v.astype(BF16)
    return high, (v - high.astype(F32)).astype(BF16)


def left(v):
    high, low = split(v)
    return jnp.concatenate([high, high, low], axis=1)


def right(v):
    high, low = split(v)
    return jnp.concatenate([high, low, high], axis=0)


def dot(a, b):
    return lax.dot_general(a, b, (((1,), (0,)), ((), ())), preferred_element_type=F32)


def kernel(
    rows_in, cols_in, count_in, features, weight_in, bias_in, tiles, cotangent_in,
    out, grad_features, grad_weight, grad_bias,
    tile_rows, tile_cols, tile_count, table_out, table_in, own_table, sib_table, feat, tile, weight, bias, cotangent,
    t_left, tt_left, w_right, wt_right,
    agg_part, core_in, half, y_in2, z_out2, z_in2, agg, out_stage, grad, s_right, chain,
    b_out, b_far, b_in, b_far_in, line, p_in, y_out, y_in4, y_sum, line_in,
    gw, w_out, x_in5, z_out5, z_in5, z_out4, z_in4, pay,
    local_sem, send_sem, recv_sem,
):
    loop, rep = lax.axis_index("loop"), lax.axis_index("rep")
    x, zl = lax.div(loop, 4), lax.rem(loop, 4)
    zh, y, c = lax.div(rep, 8), lax.rem(lax.div(rep, 2), 4), lax.rem(rep, 2)
    z = zh * 4 + zl

    def device(xx, yy, zz, cc):
        return {
            "loop": xx * 4 + lax.rem(zz, 4),
            "rep": lax.div(zz, 4) * 8 + yy * 2 + cc,
        }

    def at_x(d):
        return device(lax.rem(x + d + 4, 4), y, z, c)

    def at_y(d):
        return device(x, lax.rem(y + d + 4, 4), z, c)

    def at_z(d):
        return device(x, y, lax.rem(z + d + 8, 8), c)

    def along_a(d, dy=0):
        return device(
            lax.rem(x + (1 - c) * d + 4, 4),
            lax.rem(y + dy, 4),
            lax.rem(z + c * d + 8, 8),
            c,
        )

    def along_b(d):
        return device(
            lax.rem(x + c * d + 4, 4), y, lax.rem(z + (1 - c) * d + 8, 8), c
        )

    sibling = device(x, y, z, 1 - c)
    a, b = (1 - c) * x + c * zl, c * x + (1 - c) * zl

    def chunk(da, db):
        aa, bb = lax.rem(a + da + 4, 4), lax.rem(b + db + 4, 4)
        return (aa * (4 - 3 * c) + bb * (1 + 3 * c)) * 2

    counter = [0]
    sent = []

    def push(src, dst, to, recv=None):
        n = counter[0]
        counter[0] += 1
        copy = pltpu.make_async_remote_copy(
            src_ref=src,
            dst_ref=dst,
            send_sem=send_sem.at[n],
            recv_sem=recv_sem.at[n if recv is None else recv],
            device_id=to,
            device_id_type=pl.DeviceIdType.MESH,
        )
        copy.start()
        sent.append(copy)
        return copy

    partners = [at_x(1), at_x(2), at_x(3), at_y(1), at_y(2), at_y(3)]
    partners += [at_z(1), at_z(2), at_z(6), at_z(7), sibling]
    barrier = pltpu.get_barrier_semaphore()
    for partner in partners:
        pl.semaphore_signal(
            barrier, inc=1, device_id=partner, device_id_type=pl.DeviceIdType.MESH
        )

    own = pltpu.make_async_copy(
        features.at[pl.ds(4 * c, 4)], feat.at[pl.ds(4 * loop, 4)], local_sem.at[0]
    )
    own.start()
    slots_in = [
        pltpu.make_async_copy(src, dst, local_sem.at[9 + n])
        for n, (src, dst) in enumerate(
            ((rows_in, tile_rows), (cols_in, tile_cols), (count_in, tile_count))
        )
    ]
    for copy in slots_in:
        copy.start()
    tiles_in = pltpu.make_async_copy(tiles, tile.at[pl.ds(0, 16)], local_sem.at[2])
    tiles_in.start()
    layer_in = [
        pltpu.make_async_copy(src, dst, local_sem.at[5 + n])
        for n, (src, dst) in enumerate(
            ((weight_in, weight), (bias_in, bias), (cotangent_in, cotangent))
        )
    ]
    for copy in layer_in:
        copy.start()

    for copy in slots_in:
        copy.wait()
    table_out[...] = make_table(tile_rows, tile_cols, tile_count)
    table_local = pltpu.make_async_copy(table_out, own_table, local_sem.at[8])
    table_local.start()
    own.wait()
    pl.semaphore_wait(barrier, len(partners))

    def rows_of(da, db, first=0, pieces=4):
        return feat.at[pl.ds(2 * chunk(da, db) + first, pieces)]

    by_pieces = (0,)
    a_near = [push(rows_of(0, 0), rows_of(0, 0), along_a(d)) for d in (1, -1)]
    b_near, b_two, y_spread = {}, {}, []
    two_away = 4 * lax.div(y, 2) - 2

    def far(da, along):
        views = [rows_of(da, 0, 2 * j, 2) for j in range(2)]
        return [push(views[j], views[j], along(4 * j - 2)) for j in range(2)]

    def out_b(da):
        view = rows_of(da, 0, y, 1) if da in by_pieces else rows_of(da, 0)
        b_near[da] = [push(view, view, along_b(d)) for d in (1, -1)]
        if da in by_pieces:
            b_two[da] = [push(view, view, along_b(two_away))]
        elif da == 2:
            b_two[da] = far(da, along_b)

    def near_b(da):
        for i, d in ((0, 1), (1, -1)):
            b_near[da][i].wait_recv()
            if da in by_pieces:
                spread(da, -d)
            elif da != 2:
                view = rows_of(da, -d, 2 * i, 2)
                b_two.setdefault(da, []).append(push(view, view, along_b(d)))
        if da in by_pieces:
            b_two[da][0].wait_recv()
            spread(da, 2)

    def spread(da, db):
        view = rows_of(da, db, y, 1)
        y_spread.extend(push(view, view, at_y(d)) for d in (2, 1, 3))

    out_b(0)
    a_far = far(0, along_a)
    table_move = push(table_out, table_in, sibling)
    tiles_move = push(tiles, tile.at[pl.ds(16, 16)], sibling)

    def split_tiles(start):
        def two(n, _):
            for s in (start + 2 * n, start + 2 * n + 1):
                t_left[s] = left(tile[s])
                tt_left[s] = left(tile[s].T)
            return 0

        lax.fori_loop(0, 8, two, 0)

    near_b(0)
    for i, d in ((0, 1), (1, -1)):
        a_near[i].wait_recv()
        out_b(-d)
    for move in a_far:
        move.wait_recv()
    out_b(2)
    table_local.wait()
    table_move.wait_recv()
    table_local = pltpu.make_async_copy(table_in, sib_table, local_sem.at[3])
    table_local.start()
    tiles_in.wait()
    split_tiles(0)
    near_b(-1)
    near_b(1)
    tiles_move.wait_recv()
    split_tiles(16)
    for copy in layer_in:
        copy.wait()
    chain[16] = jnp.zeros((128, 128), F32)
    chain[33] = jnp.zeros((128, 128), F32)
    w_right[...] = right(weight[...])
    wt_right[...] = right(weight[...].T)
    table_local.wait()
    near_b(2)
    for da in (-1, 1, 2):
        if da not in by_pieces:
            for move in b_two[da]:
                move.wait_recv()
    for move in y_spread:
        move.wait_recv()

    tables = (own_table, sib_table)
    for s in range(16):
        for side, table in enumerate(tables):
            spot = 2 * lax.rem(table[0, s], 32)
            block = right(feat[pl.ds(spot, 2)].reshape(128, 128))
            product = dot(t_left[16 * side + s], block)
            chain[17 * side + s] = product + chain[17 * side + table[0, 16 + s]]
    for j in range(4):
        f = 4 * c + j
        agg_part[j] = chain[own_table[1, f]] + chain[17 + sib_table[1, f]]

    other = push(agg_part.at[pl.ds(2 * (1 - c), 2)], core_in, sibling)
    other.wait_recv()
    for j in range(2):
        half[128 * j : 128 * j + 128, :] = agg_part[2 * c + j] + core_in[j]

    def sum_z(value, z_out, z_in):
        z_out[...] = value
        swap = push(z_out, z_in, at_z(4))
        swap.wait_recv()
        return z_out[...] + z_in[...]

    def reduce_rep(part, y_in, z_out, z_in):
        moves = []
        for d in (2, 1, 3):
            there = lax.rem(y + d, 4)
            moves.append(
                push(part.at[pl.ds(there * 64, 64)], y_in.at[y], at_y(d))
            )
        y_in[y] = part[pl.ds(pl.multiple_of(y * 64, 64), 64), :]
        for move in moves:
            move.wait_recv()
        return sum_z((y_in[0] + y_in[1]) + (y_in[2] + y_in[3]), z_out, z_in)

    def gather_rep(buf, sem):
        mine = buf.at[c * 4 + y]
        moves = [(d, push(mine, mine, at_y(d))) for d in (2, 1, 3)]
        push(mine, mine, sibling, recv=sem)
        for d, move in moves[1:] + moves[:1]:
            move.wait_recv()
            got = buf.at[c * 4 + lax.rem(y - d + 4, 4)]
            push(got, got, sibling, recv=sem)
        pltpu.make_async_copy(
            buf.at[pl.ds(0, 4)], buf.at[pl.ds(0, 4)], recv_sem.at[sem]
        ).wait()

    total = reduce_rep(half, y_in2, z_out2, z_in2)
    agg[c * 4 + y] = total
    gather_rep(agg, 111)

    for r in range(4):
        rows = slice(128 * r, 128 * r + 128)
        mine = agg[2 * r : 2 * r + 2].reshape(128, 128)
        pre = dot(left(mine), w_right[...]) + bias[...]
        logistic = 1.0 / (1.0 + jnp.exp(-pre))
        out_stage[rows, :] = pre * logistic
        g = cotangent[rows, :] * logistic * (1.0 + pre * (1.0 - logistic))
        grad[rows, :] = g
        s_right[r] = right(dot(left(g), wt_right[...]))
    out_move = pltpu.make_async_copy(out_stage, out, local_sem.at[4])
    out_move.start()

    for s in range(16):
        for side, table in enumerate(tables):
            product = dot(tt_left[16 * side + s], s_right[table[0, 32 + s]])
            chain[17 * side + s] = product + chain[17 * side + table[0, 48 + s]]

    def dense(da, db, j):
        f = 64 + 32 * c + chunk(da, db) + j
        return chain[own_table[0, f]] + chain[17 + sib_table[0, f]]

    order = (2, -1, 1, 0)
    to_near, to_far = {}, {}
    for k, da in enumerate(order[:3]):
        for j in range(2):
            b_far[k, j] = dense(da, 2, j)
            to_far[k, j] = push(b_far.at[k, j], b_far_in.at[k, j], along_b(1 - 2 * j))

    y_moves = []
    for n, db in enumerate((2, -1, 1, 0)):
        for j in range(2):
            y_out[n, 2 * j : 2 * j + 2] = dense(0, db, j).reshape(2, 64, 128)
        for dy in (2, 1, 3):
            piece = lax.rem(y + dy, 4)
            y_moves.append(push(y_out.at[n, piece], y_in4.at[n, dy - 1], at_y(dy)))

    def to_next(k, da):
        for i, d in ((0, 1), (1, -1)):
            b_out[i, k, 1 - i] = dense(da, d, 1 - i)
            to_far[k, i].wait_recv()
            b_out[i, k, i] = dense(da, d, i) + b_far_in[k, i]
            to_near[k, i] = push(b_out.at[i, k], b_in.at[i, k], along_b(d))

    gw[...] = dot(left(agg[...].reshape(512, 128).T), right(grad[...]))
    w_out[0:16, :] = gw[pl.ds(pl.multiple_of((c * 4 + y) * 16, 16), 16), :]
    w_out[16:24, :] = jnp.broadcast_to(
        jnp.sum(grad[...], axis=0, keepdims=True), (8, 256)
    )
    x_in5[x] = w_out[...]
    x_moves = [push(w_out, x_in5.at[x], at_x(d)) for d in (2, 1, 3)]
    for k, da in enumerate(order[:3]):
        to_next(k, da)
    for move in y_moves:
        move.wait_recv()
    line_moves = []
    for n, d in enumerate((two_away, -1, 1, 0)):
        y_sum[n] = (y_out[n, y] + y_in4[n, 0]) + (y_in4[n, 1] + y_in4[n, 2])
        if n < 3:
            line_moves.append(push(y_sum.at[n], line_in.at[n], along_b(d)))

    pieces = []
    for k, da in enumerate(order[:3]):
        for i in range(2):
            to_near[k, i].wait_recv()
        for j in range(2):
            value = dense(da, 0, j) + (b_in[0, k, j] + b_in[1, k, j])
            line[k, 2 * j : 2 * j + 2] = value.reshape(2, 64, 128)
        for dy in (2, 1, 3, 0):
            piece = lax.rem(y + dy, 4)
            d = 4 * lax.div(piece, 2) - 2 if da == 2 else da
            pieces.append(push(line.at[k, piece], p_in.at[k, dy], along_a(d, dy)))
    for move in x_moves:
        move.wait_recv()
    z_out5[...] = (x_in5[0] + x_in5[1]) + (x_in5[2] + x_in5[3])
    z_in5[zl] = z_out5[...]
    z_moves = [push(z_out5, z_in5.at[zl], at_z(d)) for d in (2, 1, -1)]
    total = y_sum[3]
    for n in range(3):
        line_moves[n].wait_recv()
        total += line_in[n]
    for k in range(3):
        for n, dy in enumerate((2, 1, 3, 0)):
            pieces[4 * k + n].wait_recv()
            total += p_in[k, dy]
    total = sum_z(total, z_out4, z_in4)
    for move in z_moves:
        move.wait_recv()
    here = c * 4 + y
    pay[here, 0:64, :] = total
    summed = (z_in5[0] + z_in5[1]) + (z_in5[2] + z_in5[3])
    pay[here, 64:80, :] = summed[0:16, 0:128]
    pay[here, 80:96, :] = summed[0:16, 128:256]
    grad_bias[...] = summed[16:17, :]
    gather_rep(pay, 112)
    for i in range(8):
        grad_features[64 * i : 64 * i + 64, :] = pay[i, 0:64, :]
        grad_weight[16 * i : 16 * i + 16, 0:128] = pay[i, 64:80, :]
        grad_weight[16 * i : 16 * i + 16, 128:256] = pay[i, 80:96, :]
    out_move.wait()
    for copy in sent:
        copy.wait_send()


def make_table(tile_rows, tile_cols, tile_count):
    lane = lax.broadcasted_iota(jnp.int32, (1, 128), 1)
    slot, part = lax.rem(lane, 16), lax.div(lane, 16)
    spots, lines = [], []
    for s in range(16):
        col = tile_cols[s]
        side = lax.rem(lax.div(col, 2), 2)
        spots.append(side * 32 + lax.div(col, 4) * 2 + lax.rem(col, 2))
        lines.append(side * 4 + lax.rem(tile_rows[s], 4))
    spot = jnp.zeros((1, 128), jnp.int32)
    line = jnp.zeros((1, 128), jnp.int32)
    for s in range(16):
        spot = jnp.where(slot == s, spots[s], spot)
        line = jnp.where(slot == s, lines[s], line)
    by_spot = jnp.where(part >= 4, lane - 64, spot)
    limit = jnp.where(part >= 4, 16, slot)
    found = jnp.full((1, 128), 16, jnp.int32)
    found_line, last_line = found, found
    for s in range(16):
        live = tile_count[0] > s
        found = jnp.where((by_spot == spots[s]) & (limit > s) & live, s, found)
        found_line = jnp.where((line == lines[s]) & (slot > s) & live, s, found_line)
        last_line = jnp.where((lane == lines[s]) & live, s, last_line)
    table = jnp.where(part == 0, spot, found)
    table = jnp.where(part == 1, found_line, table)
    table = jnp.where(part == 2, lax.rem(line, 4), table)
    return jnp.concatenate([table, last_line], axis=0)


def finish_kernel(*refs):
    sems = refs[8]
    moves = [pltpu.make_async_copy(refs[n], refs[4 + n], sems.at[n]) for n in range(4)]
    for move in moves:
        move.start()
    for move in moves:
        move.wait()


def per_device(features, weight, bias, tile_values, tile_rows, tile_cols, tile_count, cotangent):
    vmem, hbm = pltpu.VMEM, pl.BlockSpec(memory_space=pltpu.HBM)
    in_vmem = pl.BlockSpec(memory_space=pltpu.VMEM)
    square = (128, 128)
    shapes = (
        jax.ShapeDtypeStruct((512, 256), F32),
        jax.ShapeDtypeStruct((512, 128), F32),
        jax.ShapeDtypeStruct((128, 256), F32),
        jax.ShapeDtypeStruct((1, 256), F32),
    )
    outs = pl.pallas_call(
        kernel,
        out_shape=shapes,
        in_specs=[hbm] * 8,
        out_specs=(hbm, in_vmem, in_vmem, in_vmem),
        scratch_shapes=[
            pltpu.SMEM((16,), jnp.int32),
            pltpu.SMEM((16,), jnp.int32),
            pltpu.SMEM((1,), jnp.int32),
            vmem((2, 128), jnp.int32),
            vmem((2, 128), jnp.int32),
            pltpu.SMEM((2, 128), jnp.int32),
            pltpu.SMEM((2, 128), jnp.int32),
            vmem((64, 64, 128), F32),
            vmem((32, *square), F32),
            vmem((128, 256), F32),
            vmem((1, 256), F32),
            vmem((512, 256), F32),
            vmem((32, 128, 384), BF16),
            vmem((32, 128, 384), BF16),
            vmem((384, 256), BF16),
            vmem((768, 128), BF16),
            vmem((4, *square), F32),
            vmem((2, *square), F32),
            vmem((256, 128), F32),
            vmem((4, 64, 128), F32),
            vmem((64, 128), F32),
            vmem((64, 128), F32),
            vmem((8, 64, 128), F32),
            vmem((512, 256), F32),
            vmem((512, 256), F32),
            vmem((4, 384, 128), BF16),
            vmem((34, *square), F32),
            vmem((2, 4, 2, *square), F32),
            vmem((4, 2, *square), F32),
            vmem((2, 4, 2, *square), F32),
            vmem((4, 2, *square), F32),
            vmem((3, 4, 64, 128), F32),
            vmem((3, 4, 64, 128), F32),
            vmem((4, 4, 64, 128), F32),
            vmem((4, 3, 64, 128), F32),
            vmem((4, 64, 128), F32),
            vmem((3, 64, 128), F32),
            vmem((128, 256), F32),
            vmem((24, 256), F32),
            vmem((4, 24, 256), F32),
            vmem((24, 256), F32),
            vmem((4, 24, 256), F32),
            vmem((64, 128), F32),
            vmem((64, 128), F32),
            vmem((8, 96, 128), F32),
            pltpu.SemaphoreType.DMA((12,)),
            pltpu.SemaphoreType.DMA((120,)),
            pltpu.SemaphoreType.DMA((120,)),
        ],
        compiler_params=pltpu.CompilerParams(
            collective_id=0, has_side_effects=True, vmem_limit_bytes=60 * 1024 * 1024
        ),
        cost_estimate=pl.CostEstimate(
            flops=400_000_000, bytes_accessed=4_000_000, transcendentals=131072
        ),
    )(
        tile_rows,
        tile_cols,
        tile_count,
        features.reshape(8, 64, 128),
        weight,
        bias[None, :],
        tile_values,
        cotangent,
    )
    output, grad_features, grad_weight, grad_bias = pl.pallas_call(
        finish_kernel,
        out_shape=shapes,
        in_specs=[in_vmem] * 4,
        out_specs=[hbm] * 4,
        scratch_shapes=[pltpu.SemaphoreType.DMA((4,))],
    )(*outs)
    return output, grad_features, grad_weight, grad_bias[0]


def solution(mesh):
    return jax.shard_map(
        per_device,
        mesh=mesh,
        in_specs=(
            P("loop", None),
            P(),
            P(),
            P(("loop", "rep"), None, None),
            P(("loop", "rep")),
            P(("loop", "rep")),
            P(("loop", "rep")),
            P("loop", None),
        ),
        out_specs=(P("loop", None), P("loop", None), P(), P()),
        check_vma=False,
    )
```

```python
import jax
import jax.numpy as jnp
from jax import lax
from jax.experimental import pallas as pl
from jax.experimental.pallas import tpu as pltpu
from jax.sharding import PartitionSpec as P

F32, BF16 = jnp.float32, jnp.bfloat16


def split(v):
    high = v.astype(BF16)
    return high, (v - high.astype(F32)).astype(BF16)


def left(v):
    high, low = split(v)
    return jnp.concatenate([high, high, low], axis=1)


def right(v):
    high, low = split(v)
    return jnp.concatenate([high, low, high], axis=0)


def dot(a, b):
    return lax.dot_general(a, b, (((1,), (0,)), ((), ())), preferred_element_type=F32)


def kernel(
    rows_in, cols_in, count_in, features, weight_in, bias_in, tiles, cotangent_in,
    out, grad_features, grad_weight, grad_bias,
    tile_rows, tile_cols, tile_count, table_out, table_in, own_table, sib_table, feat, tile, weight, bias, cotangent,
    t_left, tt_left, w_right, wt_right,
    agg_part, core_in, half, y_in2, z_out2, z_in2, agg, out_stage, grad, s_right, chain,
    b_out, b_far, b_in, b_far_in, line, p_in, y_out, y_in4, y_sum, line_in,
    gw, w_out, x_in5, z_out5, z_in5, z_out4, z_in4, pay,
    local_sem, send_sem, recv_sem,
):
    loop, rep = lax.axis_index("loop"), lax.axis_index("rep")
    x, zl = lax.div(loop, 4), lax.rem(loop, 4)
    zh, y, c = lax.div(rep, 8), lax.rem(lax.div(rep, 2), 4), lax.rem(rep, 2)
    z = zh * 4 + zl

    def device(xx, yy, zz, cc):
        return {
            "loop": xx * 4 + lax.rem(zz, 4),
            "rep": lax.div(zz, 4) * 8 + yy * 2 + cc,
        }

    def at_x(d):
        return device(lax.rem(x + d + 4, 4), y, z, c)

    def at_y(d):
        return device(x, lax.rem(y + d + 4, 4), z, c)

    def at_z(d):
        return device(x, y, lax.rem(z + d + 8, 8), c)

    def along_a(d, dy=0):
        return device(
            lax.rem(x + (1 - c) * d + 4, 4),
            lax.rem(y + dy, 4),
            lax.rem(z + c * d + 8, 8),
            c,
        )

    def along_b(d):
        return device(
            lax.rem(x + c * d + 4, 4), y, lax.rem(z + (1 - c) * d + 8, 8), c
        )

    sibling = device(x, y, z, 1 - c)
    a, b = (1 - c) * x + c * zl, c * x + (1 - c) * zl

    def chunk(da, db):
        aa, bb = lax.rem(a + da + 4, 4), lax.rem(b + db + 4, 4)
        return (aa * (4 - 3 * c) + bb * (1 + 3 * c)) * 2

    counter = [0]
    sent = []

    def push(src, dst, to, recv=None):
        n = counter[0]
        counter[0] += 1
        copy = pltpu.make_async_remote_copy(
            src_ref=src,
            dst_ref=dst,
            send_sem=send_sem.at[n],
            recv_sem=recv_sem.at[n if recv is None else recv],
            device_id=to,
            device_id_type=pl.DeviceIdType.MESH,
        )
        copy.start()
        sent.append(copy)
        return copy

    partners = [at_x(1), at_x(2), at_x(3), at_y(1), at_y(2), at_y(3)]
    partners += [at_z(1), at_z(2), at_z(6), at_z(7), sibling]
    barrier = pltpu.get_barrier_semaphore()
    for partner in partners:
        pl.semaphore_signal(
            barrier, inc=1, device_id=partner, device_id_type=pl.DeviceIdType.MESH
        )

    own = pltpu.make_async_copy(
        features.at[pl.ds(4 * c, 4)], feat.at[pl.ds(4 * loop, 4)], local_sem.at[0]
    )
    own.start()
    slots_in = [
        pltpu.make_async_copy(src, dst, local_sem.at[9 + n])
        for n, (src, dst) in enumerate(
            ((rows_in, tile_rows), (cols_in, tile_cols), (count_in, tile_count))
        )
    ]
    for copy in slots_in:
        copy.start()
    tiles_in = pltpu.make_async_copy(tiles, tile.at[pl.ds(0, 16)], local_sem.at[2])
    tiles_in.start()
    layer_in = [
        pltpu.make_async_copy(src, dst, local_sem.at[5 + n])
        for n, (src, dst) in enumerate(
            ((weight_in, weight), (bias_in, bias), (cotangent_in, cotangent))
        )
    ]
    for copy in layer_in:
        copy.start()

    for copy in slots_in:
        copy.wait()
    table_out[...] = make_table(tile_rows, tile_cols, tile_count)
    table_local = pltpu.make_async_copy(table_out, own_table, local_sem.at[8])
    table_local.start()
    own.wait()
    pl.semaphore_wait(barrier, len(partners))

    def rows_of(da, db, first=0, pieces=4):
        return feat.at[pl.ds(2 * chunk(da, db) + first, pieces)]

    by_pieces = (0,)
    a_near = [push(rows_of(0, 0), rows_of(0, 0), along_a(d)) for d in (1, -1)]
    b_near, b_two, y_spread = {}, {}, []
    two_away = 4 * lax.div(y, 2) - 2

    def far(da, along):
        views = [rows_of(da, 0, 2 * j, 2) for j in range(2)]
        return [push(views[j], views[j], along(4 * j - 2)) for j in range(2)]

    def out_b(da):
        view = rows_of(da, 0, y, 1) if da in by_pieces else rows_of(da, 0)
        b_near[da] = [push(view, view, along_b(d)) for d in (1, -1)]
        if da in by_pieces:
            b_two[da] = [push(view, view, along_b(two_away))]
        elif da == 2:
            b_two[da] = far(da, along_b)

    def near_b(da):
        for i, d in ((0, 1), (1, -1)):
            b_near[da][i].wait_recv()
            if da in by_pieces:
                spread(da, -d)
            elif da != 2:
                view = rows_of(da, -d, 2 * i, 2)
                b_two.setdefault(da, []).append(push(view, view, along_b(d)))
        if da in by_pieces:
            b_two[da][0].wait_recv()
            spread(da, 2)

    def spread(da, db):
        view = rows_of(da, db, y, 1)
        y_spread.extend(push(view, view, at_y(d)) for d in (2, 1, 3))

    out_b(0)
    a_far = far(0, along_a)
    table_move = push(table_out, table_in, sibling)
    tiles_move = push(tiles, tile.at[pl.ds(16, 16)], sibling)

    def split_tiles(start):
        def two(n, _):
            for s in (start + 2 * n, start + 2 * n + 1):
                t_left[s] = left(tile[s])
                tt_left[s] = left(tile[s].T)
            return 0

        lax.fori_loop(0, 8, two, 0)

    near_b(0)
    for i, d in ((0, 1), (1, -1)):
        a_near[i].wait_recv()
        out_b(-d)
    for move in a_far:
        move.wait_recv()
    out_b(2)
    table_local.wait()
    table_move.wait_recv()
    table_local = pltpu.make_async_copy(table_in, sib_table, local_sem.at[3])
    table_local.start()
    tiles_in.wait()
    split_tiles(0)
    near_b(-1)
    near_b(1)
    tiles_move.wait_recv()
    split_tiles(16)
    for copy in layer_in:
        copy.wait()
    chain[16] = jnp.zeros((128, 128), F32)
    chain[33] = jnp.zeros((128, 128), F32)
    w_right[...] = right(weight[...])
    wt_right[...] = right(weight[...].T)
    table_local.wait()
    near_b(2)
    for da in (-1, 1, 2):
        if da not in by_pieces:
            for move in b_two[da]:
                move.wait_recv()
    for move in y_spread:
        move.wait_recv()

    tables = (own_table, sib_table)
    for s in range(16):
        for side, table in enumerate(tables):
            spot = 2 * lax.rem(table[0, s], 32)
            block = right(feat[pl.ds(spot, 2)].reshape(128, 128))
            product = dot(t_left[16 * side + s], block)
            chain[17 * side + s] = product + chain[17 * side + table[0, 16 + s]]
    for j in range(4):
        f = 4 * c + j
        agg_part[j] = chain[own_table[1, f]] + chain[17 + sib_table[1, f]]

    other = push(agg_part.at[pl.ds(2 * (1 - c), 2)], core_in, sibling)
    other.wait_recv()
    for j in range(2):
        half[128 * j : 128 * j + 128, :] = agg_part[2 * c + j] + core_in[j]

    def sum_z(value, z_out, z_in):
        z_out[...] = value
        earlier = len(sent)
        swap = push(z_out, z_in, at_z(4))
        for copy in sent[:earlier]:
            copy.wait_send()
        del sent[:earlier]
        swap.wait_recv()
        return z_out[...] + z_in[...]

    def reduce_rep(part, y_in, z_out, z_in):
        moves = []
        for d in (2, 1, 3):
            there = lax.rem(y + d, 4)
            moves.append(
                push(part.at[pl.ds(there * 64, 64)], y_in.at[y], at_y(d))
            )
        y_in[y] = part[pl.ds(pl.multiple_of(y * 64, 64), 64), :]
        for move in moves:
            move.wait_recv()
        return sum_z((y_in[0] + y_in[1]) + (y_in[2] + y_in[3]), z_out, z_in)

    def gather_rep(buf, sem):
        mine = buf.at[c * 4 + y]
        moves = [(d, push(mine, mine, at_y(d))) for d in (2, 1, 3)]
        push(mine, mine, sibling, recv=sem)
        for d, move in moves[1:] + moves[:1]:
            move.wait_recv()
            got = buf.at[c * 4 + lax.rem(y - d + 4, 4)]
            push(got, got, sibling, recv=sem)
        return pltpu.make_async_copy(
            buf.at[pl.ds(0, 4)], buf.at[pl.ds(0, 4)], recv_sem.at[sem]
        )

    total = reduce_rep(half, y_in2, z_out2, z_in2)
    agg[c * 4 + y] = total
    others = gather_rep(agg, 111)

    def layer(r):
        rows = pl.ds(pl.multiple_of(128 * r, 128), 128)
        mine = agg[pl.ds(2 * r, 2)].reshape(128, 128)
        pre = dot(left(mine), w_right[...]) + bias[...]
        logistic = 1.0 / (1.0 + jnp.exp(-pre))
        out_stage[rows, :] = pre * logistic
        g = cotangent[rows, :] * logistic * (1.0 + pre * (1.0 - logistic))
        grad[rows, :] = g
        s_right[r] = right(dot(left(g), wt_right[...]))

    layer(2 * c)
    layer(2 * c + 1)
    others.wait()
    layer(2 - 2 * c)
    layer(3 - 2 * c)
    out_move = pltpu.make_async_copy(out_stage, out, local_sem.at[4])
    out_move.start()

    for s in range(16):
        for side, table in enumerate(tables):
            product = dot(tt_left[16 * side + s], s_right[table[0, 32 + s]])
            chain[17 * side + s] = product + chain[17 * side + table[0, 48 + s]]

    def dense(da, db, j):
        f = 64 + 32 * c + chunk(da, db) + j
        return chain[own_table[0, f]] + chain[17 + sib_table[0, f]]

    order = (2, -1, 1, 0)
    to_near, to_far = {}, {}
    for k, da in enumerate(order[:3]):
        for j in range(2):
            b_far[k, j] = dense(da, 2, j)
            to_far[k, j] = push(b_far.at[k, j], b_far_in.at[k, j], along_b(1 - 2 * j))

    y_moves = []
    for n, db in enumerate((2, -1, 1, 0)):
        for j in range(2):
            y_out[n, 2 * j : 2 * j + 2] = dense(0, db, j).reshape(2, 64, 128)
        for dy in (2, 1, 3):
            piece = lax.rem(y + dy, 4)
            y_moves.append(push(y_out.at[n, piece], y_in4.at[n, dy - 1], at_y(dy)))

    def to_next(k, da):
        for i, d in ((0, 1), (1, -1)):
            b_out[i, k, 1 - i] = dense(da, d, 1 - i)
            to_far[k, i].wait_recv()
            b_out[i, k, i] = dense(da, d, i) + b_far_in[k, i]
            to_near[k, i] = push(b_out.at[i, k], b_in.at[i, k], along_b(d))

    gw[...] = dot(left(agg[...].reshape(512, 128).T), right(grad[...]))
    w_out[0:16, :] = gw[pl.ds(pl.multiple_of((c * 4 + y) * 16, 16), 16), :]
    w_out[16:24, :] = jnp.broadcast_to(
        jnp.sum(grad[...], axis=0, keepdims=True), (8, 256)
    )
    x_in5[x] = w_out[...]
    x_moves = [push(w_out, x_in5.at[x], at_x(d)) for d in (2, 1, 3)]
    for k, da in enumerate(order[:3]):
        to_next(k, da)
    for move in y_moves:
        move.wait_recv()
    line_moves = []
    for n, d in enumerate((two_away, -1, 1, 0)):
        y_sum[n] = (y_out[n, y] + y_in4[n, 0]) + (y_in4[n, 1] + y_in4[n, 2])
        if n < 3:
            line_moves.append(push(y_sum.at[n], line_in.at[n], along_b(d)))

    pieces = []
    for k, da in enumerate(order[:3]):
        for i in range(2):
            to_near[k, i].wait_recv()
        for j in range(2):
            value = dense(da, 0, j) + (b_in[0, k, j] + b_in[1, k, j])
            line[k, 2 * j : 2 * j + 2] = value.reshape(2, 64, 128)
        for dy in (2, 1, 3, 0):
            piece = lax.rem(y + dy, 4)
            d = 4 * lax.div(piece, 2) - 2 if da == 2 else da
            pieces.append(push(line.at[k, piece], p_in.at[k, dy], along_a(d, dy)))
    for move in x_moves:
        move.wait_recv()
    z_out5[...] = (x_in5[0] + x_in5[1]) + (x_in5[2] + x_in5[3])
    z_in5[zl] = z_out5[...]
    z_moves = [push(z_out5, z_in5.at[zl], at_z(d)) for d in (2, 1, -1)]
    total = y_sum[3]
    for n in range(3):
        line_moves[n].wait_recv()
        total += line_in[n]
    for k in range(3):
        for n, dy in enumerate((2, 1, 3, 0)):
            pieces[4 * k + n].wait_recv()
            total += p_in[k, dy]
    total = sum_z(total, z_out4, z_in4)
    for move in z_moves:
        move.wait_recv()
    here = c * 4 + y
    pay[here, 0:64, :] = total
    summed = (z_in5[0] + z_in5[1]) + (z_in5[2] + z_in5[3])
    pay[here, 64:80, :] = summed[0:16, 0:128]
    pay[here, 80:96, :] = summed[0:16, 128:256]
    grad_bias[...] = summed[16:17, :]
    gather_rep(pay, 112).wait()
    for i in range(8):
        grad_features[64 * i : 64 * i + 64, :] = pay[i, 0:64, :]
        grad_weight[16 * i : 16 * i + 16, 0:128] = pay[i, 64:80, :]
        grad_weight[16 * i : 16 * i + 16, 128:256] = pay[i, 80:96, :]
    out_move.wait()
    for copy in sent:
        copy.wait_send()


def make_table(tile_rows, tile_cols, tile_count):
    lane = lax.broadcasted_iota(jnp.int32, (1, 128), 1)
    slot, part = lax.rem(lane, 16), lax.div(lane, 16)
    spots, lines = [], []
    for s in range(16):
        col = tile_cols[s]
        side = lax.rem(lax.div(col, 2), 2)
        spots.append(side * 32 + lax.div(col, 4) * 2 + lax.rem(col, 2))
        lines.append(side * 4 + lax.rem(tile_rows[s], 4))
    spot = jnp.zeros((1, 128), jnp.int32)
    line = jnp.zeros((1, 128), jnp.int32)
    for s in range(16):
        spot = jnp.where(slot == s, spots[s], spot)
        line = jnp.where(slot == s, lines[s], line)
    by_spot = jnp.where(part >= 4, lane - 64, spot)
    limit = jnp.where(part >= 4, 16, slot)
    found = jnp.full((1, 128), 16, jnp.int32)
    found_line, last_line = found, found
    for s in range(16):
        live = tile_count[0] > s
        found = jnp.where((by_spot == spots[s]) & (limit > s) & live, s, found)
        found_line = jnp.where((line == lines[s]) & (slot > s) & live, s, found_line)
        last_line = jnp.where((lane == lines[s]) & live, s, last_line)
    table = jnp.where(part == 0, spot, found)
    table = jnp.where(part == 1, found_line, table)
    table = jnp.where(part == 2, lax.rem(line, 4), table)
    return jnp.concatenate([table, last_line], axis=0)


def finish_kernel(*refs):
    sources, results, through, sems = refs[:4], refs[4:8], refs[8:12], refs[12]
    moves = [
        (
            pltpu.make_async_copy(sources[n], through[n], sems.at[n]),
            pltpu.make_async_copy(through[n], results[n], sems.at[n]),
        )
        for n in range(4)
    ]
    for read, _ in moves:
        read.start()
    for read, write in moves:
        read.wait()
        write.start()
    for _, write in moves:
        write.wait()


def per_device(features, weight, bias, tile_values, tile_rows, tile_cols, tile_count, cotangent):
    vmem, hbm = pltpu.VMEM, pl.BlockSpec(memory_space=pltpu.HBM)
    in_vmem = pl.BlockSpec(memory_space=pltpu.VMEM)
    square = (128, 128)
    shapes = (
        jax.ShapeDtypeStruct((512, 256), F32),
        jax.ShapeDtypeStruct((512, 128), F32),
        jax.ShapeDtypeStruct((128, 256), F32),
        jax.ShapeDtypeStruct((1, 256), F32),
    )
    outs = pl.pallas_call(
        kernel,
        out_shape=shapes,
        in_specs=[hbm] * 8,
        out_specs=(hbm, in_vmem, in_vmem, in_vmem),
        scratch_shapes=[
            pltpu.SMEM((16,), jnp.int32),
            pltpu.SMEM((16,), jnp.int32),
            pltpu.SMEM((1,), jnp.int32),
            vmem((2, 128), jnp.int32),
            vmem((2, 128), jnp.int32),
            pltpu.SMEM((2, 128), jnp.int32),
            pltpu.SMEM((2, 128), jnp.int32),
            vmem((64, 64, 128), F32),
            vmem((32, *square), F32),
            vmem((128, 256), F32),
            vmem((1, 256), F32),
            vmem((512, 256), F32),
            vmem((32, 128, 384), BF16),
            vmem((32, 128, 384), BF16),
            vmem((384, 256), BF16),
            vmem((768, 128), BF16),
            vmem((4, *square), F32),
            vmem((2, *square), F32),
            vmem((256, 128), F32),
            vmem((4, 64, 128), F32),
            vmem((64, 128), F32),
            vmem((64, 128), F32),
            vmem((8, 64, 128), F32),
            vmem((512, 256), F32),
            vmem((512, 256), F32),
            vmem((4, 384, 128), BF16),
            vmem((34, *square), F32),
            vmem((2, 4, 2, *square), F32),
            vmem((4, 2, *square), F32),
            vmem((2, 4, 2, *square), F32),
            vmem((4, 2, *square), F32),
            vmem((3, 4, 64, 128), F32),
            vmem((3, 4, 64, 128), F32),
            vmem((4, 4, 64, 128), F32),
            vmem((4, 3, 64, 128), F32),
            vmem((4, 64, 128), F32),
            vmem((3, 64, 128), F32),
            vmem((128, 256), F32),
            vmem((24, 256), F32),
            vmem((4, 24, 256), F32),
            vmem((24, 256), F32),
            vmem((4, 24, 256), F32),
            vmem((64, 128), F32),
            vmem((64, 128), F32),
            vmem((8, 96, 128), F32),
            pltpu.SemaphoreType.DMA((12,)),
            pltpu.SemaphoreType.DMA((113,)),
            pltpu.SemaphoreType.DMA((113,)),
        ],
        compiler_params=pltpu.CompilerParams(
            collective_id=0, has_side_effects=True, vmem_limit_bytes=60 * 1024 * 1024
        ),
        cost_estimate=pl.CostEstimate(
            flops=400_000_000, bytes_accessed=4_000_000, transcendentals=131072
        ),
    )(
        tile_rows,
        tile_cols,
        tile_count,
        features.reshape(8, 64, 128),
        weight,
        bias[None, :],
        tile_values,
        cotangent,
    )
    output, grad_features, grad_weight, grad_bias = pl.pallas_call(
        finish_kernel,
        out_shape=shapes,
        in_specs=[hbm] * 4,
        out_specs=[hbm] * 4,
        scratch_shapes=[vmem(v.shape, F32) for v in shapes]
        + [pltpu.SemaphoreType.DMA((4,))],
    )(*outs)
    return output, grad_features, grad_weight, grad_bias[0]


def solution(mesh):
    return jax.shard_map(
        per_device,
        mesh=mesh,
        in_specs=(
            P("loop", None),
            P(),
            P(),
            P(("loop", "rep"), None, None),
            P(("loop", "rep")),
            P(("loop", "rep")),
            P(("loop", "rep")),
            P("loop", None),
        ),
        out_specs=(P("loop", None), P("loop", None), P(), P()),
        check_vma=False,
    )
```

```python
import jax
import jax.numpy as jnp
from jax import lax
from jax.experimental import pallas as pl
from jax.experimental.pallas import tpu as pltpu
from jax.sharding import PartitionSpec as P

F32, BF16 = jnp.float32, jnp.bfloat16


def split(v):
    high = v.astype(BF16)
    return high, (v - high.astype(F32)).astype(BF16)


def left(v):
    high, low = split(v)
    return jnp.concatenate([high, high, low], axis=1)


def right(v):
    high, low = split(v)
    return jnp.concatenate([high, low, high], axis=0)


def dot(a, b):
    return lax.dot_general(a, b, (((1,), (0,)), ((), ())), preferred_element_type=F32)


def kernel(
    rows_in, cols_in, count_in, features, weight_in, bias_in, tiles, cotangent_in,
    out, grad_features, grad_weight, grad_bias,
    tile_rows, tile_cols, tile_count, table_out, table_in, own_table, sib_table, feat, tile, weight, bias, cotangent,
    t_left, tt_left, w_right, wt_right,
    agg_part, core_in, half, y_in2, z_out2, z_in2, agg, out_stage, grad, s_right, chain,
    b_out, b_far, b_in, b_far_in, line, p_in, y_out, y_in4, y_sum, line_in,
    gw, w_out, x_in5, z_out5, z_in5, z_out4, z_in4, pay, pay_w,
    local_sem, send_sem, recv_sem,
):
    loop, rep = lax.axis_index("loop"), lax.axis_index("rep")
    x, zl = lax.div(loop, 4), lax.rem(loop, 4)
    zh, y, c = lax.div(rep, 8), lax.rem(lax.div(rep, 2), 4), lax.rem(rep, 2)
    z = zh * 4 + zl

    def device(xx, yy, zz, cc):
        return {
            "loop": xx * 4 + lax.rem(zz, 4),
            "rep": lax.div(zz, 4) * 8 + yy * 2 + cc,
        }

    def at_x(d):
        return device(lax.rem(x + d + 4, 4), y, z, c)

    def at_y(d):
        return device(x, lax.rem(y + d + 4, 4), z, c)

    def at_z(d):
        return device(x, y, lax.rem(z + d + 8, 8), c)

    def along_a(d, dy=0):
        return device(
            lax.rem(x + (1 - c) * d + 4, 4),
            lax.rem(y + dy, 4),
            lax.rem(z + c * d + 8, 8),
            c,
        )

    def along_b(d):
        return device(
            lax.rem(x + c * d + 4, 4), y, lax.rem(z + (1 - c) * d + 8, 8), c
        )

    sibling = device(x, y, z, 1 - c)
    a, b = (1 - c) * x + c * zl, c * x + (1 - c) * zl

    def chunk(da, db):
        aa, bb = lax.rem(a + da + 4, 4), lax.rem(b + db + 4, 4)
        return (aa * (4 - 3 * c) + bb * (1 + 3 * c)) * 2

    counter = [0]
    sent = []

    def push(src, dst, to, recv=None):
        n = counter[0]
        counter[0] += 1
        copy = pltpu.make_async_remote_copy(
            src_ref=src,
            dst_ref=dst,
            send_sem=send_sem.at[n],
            recv_sem=recv_sem.at[n if recv is None else recv],
            device_id=to,
            device_id_type=pl.DeviceIdType.MESH,
        )
        copy.start()
        sent.append(copy)
        return copy

    partners = [at_x(1), at_x(2), at_x(3), at_y(1), at_y(2), at_y(3)]
    partners += [at_z(1), at_z(2), at_z(6), at_z(7), sibling]
    barrier = pltpu.get_barrier_semaphore()
    for partner in partners:
        pl.semaphore_signal(
            barrier, inc=1, device_id=partner, device_id_type=pl.DeviceIdType.MESH
        )

    own = pltpu.make_async_copy(
        features.at[pl.ds(4 * c, 4)], feat.at[pl.ds(4 * loop, 4)], local_sem.at[0]
    )
    own.start()
    slots_in = [
        pltpu.make_async_copy(src, dst, local_sem.at[9 + n])
        for n, (src, dst) in enumerate(
            ((rows_in, tile_rows), (cols_in, tile_cols), (count_in, tile_count))
        )
    ]
    for copy in slots_in:
        copy.start()
    tiles_in = pltpu.make_async_copy(tiles, tile.at[pl.ds(0, 16)], local_sem.at[2])
    tiles_in.start()
    layer_in = [
        pltpu.make_async_copy(src, dst, local_sem.at[5 + n])
        for n, (src, dst) in enumerate(
            ((weight_in, weight), (bias_in, bias), (cotangent_in, cotangent))
        )
    ]
    for copy in layer_in:
        copy.start()

    for copy in slots_in:
        copy.wait()
    table_out[...] = make_table(tile_rows, tile_cols, tile_count)
    table_local = pltpu.make_async_copy(table_out, own_table, local_sem.at[8])
    table_local.start()
    own.wait()
    pl.semaphore_wait(barrier, len(partners))

    def rows_of(da, db, first=0, pieces=4):
        return feat.at[pl.ds(2 * chunk(da, db) + first, pieces)]

    by_pieces = (0,)
    a_near = [push(rows_of(0, 0), rows_of(0, 0), along_a(d)) for d in (1, -1)]
    b_near, b_two, y_spread = {}, {}, []
    two_away = 4 * lax.div(y, 2) - 2

    def far(da, along):
        views = [rows_of(da, 0, 2 * j, 2) for j in range(2)]
        return [push(views[j], views[j], along(4 * j - 2)) for j in range(2)]

    def out_b(da):
        view = rows_of(da, 0, y, 1) if da in by_pieces else rows_of(da, 0)
        b_near[da] = [push(view, view, along_b(d)) for d in (1, -1)]
        if da in by_pieces:
            b_two[da] = [push(view, view, along_b(two_away))]
        elif da == 2:
            b_two[da] = far(da, along_b)

    def near_b(da):
        for i, d in ((0, 1), (1, -1)):
            b_near[da][i].wait_recv()
            if da in by_pieces:
                spread(da, -d)
            elif da != 2:
                view = rows_of(da, -d, 2 * i, 2)
                b_two.setdefault(da, []).append(push(view, view, along_b(d)))
        if da in by_pieces:
            b_two[da][0].wait_recv()
            spread(da, 2)

    def spread(da, db):
        view = rows_of(da, db, y, 1)
        y_spread.extend(push(view, view, at_y(d)) for d in (2, 1, 3))

    out_b(0)
    a_far = far(0, along_a)
    table_move = push(table_out, table_in, sibling)
    tiles_move = push(tiles, tile.at[pl.ds(16, 16)], sibling)

    def split_tiles(start):
        def two(n, _):
            for s in (start + 2 * n, start + 2 * n + 1):
                t_left[s] = left(tile[s])
                tt_left[s] = left(tile[s].T)
            return 0

        lax.fori_loop(0, 8, two, 0)

    near_b(0)
    for i, d in ((0, 1), (1, -1)):
        a_near[i].wait_recv()
        out_b(-d)
    for move in a_far:
        move.wait_recv()
    out_b(2)
    table_local.wait()
    table_move.wait_recv()
    table_local = pltpu.make_async_copy(table_in, sib_table, local_sem.at[3])
    table_local.start()
    tiles_in.wait()
    split_tiles(0)
    near_b(-1)
    near_b(1)
    tiles_move.wait_recv()
    split_tiles(16)
    for copy in layer_in:
        copy.wait()
    chain[16] = jnp.zeros((128, 128), F32)
    chain[33] = jnp.zeros((128, 128), F32)
    w_right[...] = right(weight[...])
    wt_right[...] = right(weight[...].T)
    table_local.wait()
    near_b(2)
    for da in (-1, 1, 2):
        if da not in by_pieces:
            for move in b_two[da]:
                move.wait_recv()
    for move in y_spread:
        move.wait_recv()

    tables = (own_table, sib_table)
    for s in range(16):
        for side, table in enumerate(tables):
            spot = 2 * lax.rem(table[0, s], 32)
            block = right(feat[pl.ds(spot, 2)].reshape(128, 128))
            product = dot(t_left[16 * side + s], block)
            chain[17 * side + s] = product + chain[17 * side + table[0, 16 + s]]
    for j in range(4):
        f = 4 * c + j
        agg_part[j] = chain[own_table[1, f]] + chain[17 + sib_table[1, f]]

    other = push(agg_part.at[pl.ds(2 * (1 - c), 2)], core_in, sibling)
    other.wait_recv()
    for j in range(2):
        half[128 * j : 128 * j + 128, :] = agg_part[2 * c + j] + core_in[j]

    def sum_z(value, z_out, z_in, meanwhile=None):
        z_out[...] = value
        earlier = len(sent)
        swap = push(z_out, z_in, at_z(4))
        for copy in sent[:earlier]:
            copy.wait_send()
        del sent[:earlier]
        begun = meanwhile() if meanwhile else None
        swap.wait_recv()
        if meanwhile:
            return z_out[...] + z_in[...], begun
        return z_out[...] + z_in[...]

    def reduce_rep(part, y_in, z_out, z_in):
        moves = []
        for d in (2, 1, 3):
            there = lax.rem(y + d, 4)
            moves.append(
                push(part.at[pl.ds(there * 64, 64)], y_in.at[y], at_y(d))
            )
        y_in[y] = part[pl.ds(pl.multiple_of(y * 64, 64), 64), :]
        for move in moves:
            move.wait_recv()
        return sum_z((y_in[0] + y_in[1]) + (y_in[2] + y_in[3]), z_out, z_in)

    def gather_start(buf, sem):
        mine = buf.at[c * 4 + y]
        moves = [(d, push(mine, mine, at_y(d))) for d in (2, 1, 3)]
        push(mine, mine, sibling, recv=sem)
        return moves

    def gather_rep(buf, sem, moves=None):
        if moves is None:
            moves = gather_start(buf, sem)
        for d, move in moves[1:] + moves[:1]:
            move.wait_recv()
            got = buf.at[c * 4 + lax.rem(y - d + 4, 4)]
            push(got, got, sibling, recv=sem)
        return pltpu.make_async_copy(
            buf.at[pl.ds(0, 4)], buf.at[pl.ds(0, 4)], recv_sem.at[sem]
        )

    total = reduce_rep(half, y_in2, z_out2, z_in2)
    agg[c * 4 + y] = total
    others = gather_rep(agg, 111)

    def layer(r):
        rows = pl.ds(pl.multiple_of(128 * r, 128), 128)
        mine = agg[pl.ds(2 * r, 2)].reshape(128, 128)
        pre = dot(left(mine), w_right[...]) + bias[...]
        logistic = 1.0 / (1.0 + jnp.exp(-pre))
        out_stage[rows, :] = pre * logistic
        g = cotangent[rows, :] * logistic * (1.0 + pre * (1.0 - logistic))
        grad[rows, :] = g
        s_right[r] = right(dot(left(g), wt_right[...]))

    layer(2 * c)
    layer(2 * c + 1)
    others.wait()
    layer(2 - 2 * c)
    layer(3 - 2 * c)
    out_move = pltpu.make_async_copy(out_stage, out, local_sem.at[4])
    out_move.start()

    for s in range(16):
        for side, table in enumerate(tables):
            product = dot(tt_left[16 * side + s], s_right[table[0, 32 + s]])
            chain[17 * side + s] = product + chain[17 * side + table[0, 48 + s]]

    def dense(da, db, j):
        f = 64 + 32 * c + chunk(da, db) + j
        return chain[own_table[0, f]] + chain[17 + sib_table[0, f]]

    order = (2, -1, 1, 0)
    to_near, to_far = {}, {}
    for k, da in enumerate(order[:3]):
        for j in range(2):
            b_far[k, j] = dense(da, 2, j)
            to_far[k, j] = push(b_far.at[k, j], b_far_in.at[k, j], along_b(1 - 2 * j))

    y_moves = []
    for n, db in enumerate((2, -1, 1, 0)):
        for j in range(2):
            y_out[n, 2 * j : 2 * j + 2] = dense(0, db, j).reshape(2, 64, 128)
        for dy in (2, 1, 3):
            piece = lax.rem(y + dy, 4)
            y_moves.append(push(y_out.at[n, piece], y_in4.at[n, dy - 1], at_y(dy)))

    def to_next(k, da):
        for i, d in ((0, 1), (1, -1)):
            b_out[i, k, 1 - i] = dense(da, d, 1 - i)
            to_far[k, i].wait_recv()
            b_out[i, k, i] = dense(da, d, i) + b_far_in[k, i]
            to_near[k, i] = push(b_out.at[i, k], b_in.at[i, k], along_b(d))

    gw[...] = dot(left(agg[...].reshape(512, 128).T), right(grad[...]))
    w_out[0:16, :] = gw[pl.ds(pl.multiple_of((c * 4 + y) * 16, 16), 16), :]
    w_out[16:24, :] = jnp.broadcast_to(
        jnp.sum(grad[...], axis=0, keepdims=True), (8, 256)
    )
    x_in5[x] = w_out[...]
    x_moves = [push(w_out, x_in5.at[x], at_x(d)) for d in (2, 1, 3)]
    for k, da in enumerate(order[:3]):
        to_next(k, da)
    for move in y_moves:
        move.wait_recv()
    line_moves = []
    for n, d in enumerate((two_away, -1, 1, 0)):
        y_sum[n] = (y_out[n, y] + y_in4[n, 0]) + (y_in4[n, 1] + y_in4[n, 2])
        if n < 3:
            line_moves.append(push(y_sum.at[n], line_in.at[n], along_b(d)))

    pieces = []
    for k, da in enumerate(order[:3]):
        for i in range(2):
            to_near[k, i].wait_recv()
        for j in range(2):
            value = dense(da, 0, j) + (b_in[0, k, j] + b_in[1, k, j])
            line[k, 2 * j : 2 * j + 2] = value.reshape(2, 64, 128)
        for dy in (2, 1, 3, 0):
            piece = lax.rem(y + dy, 4)
            d = 4 * lax.div(piece, 2) - 2 if da == 2 else da
            pieces.append(push(line.at[k, piece], p_in.at[k, dy], along_a(d, dy)))
    for move in x_moves:
        move.wait_recv()
    z_out5[...] = (x_in5[0] + x_in5[1]) + (x_in5[2] + x_in5[3])
    z_in5[zl] = z_out5[...]
    z_moves = [push(z_out5, z_in5.at[zl], at_z(d)) for d in (2, 1, -1)]
    total = y_sum[3]
    for n in range(3):
        line_moves[n].wait_recv()
        total += line_in[n]
    for k in range(3):
        for n, dy in enumerate((2, 1, 3, 0)):
            pieces[4 * k + n].wait_recv()
            total += p_in[k, dy]
    here = c * 4 + y

    def weight_part():
        for move in z_moves:
            move.wait_recv()
        summed = (z_in5[0] + z_in5[1]) + (z_in5[2] + z_in5[3])
        pay_w[here, 0:16, :] = summed[0:16, 0:128]
        pay_w[here, 16:32, :] = summed[0:16, 128:256]
        grad_bias[...] = summed[16:17, :]
        return gather_start(pay_w, 110)

    total, begun = sum_z(total, z_out4, z_in4, weight_part)
    pay[here] = total
    moves = gather_start(pay, 112)
    weight_others = gather_rep(pay_w, 110, begun)
    features_others = gather_rep(pay, 112, moves)
    weight_others.wait()
    features_others.wait()
    for i in range(8):
        grad_features[64 * i : 64 * i + 64, :] = pay[i]
        grad_weight[16 * i : 16 * i + 16, 0:128] = pay_w[i, 0:16, :]
        grad_weight[16 * i : 16 * i + 16, 128:256] = pay_w[i, 16:32, :]
    out_move.wait()
    for copy in sent:
        copy.wait_send()


def make_table(tile_rows, tile_cols, tile_count):
    lane = lax.broadcasted_iota(jnp.int32, (1, 128), 1)
    slot, part = lax.rem(lane, 16), lax.div(lane, 16)
    spots, lines = [], []
    for s in range(16):
        col = tile_cols[s]
        side = lax.rem(lax.div(col, 2), 2)
        spots.append(side * 32 + lax.div(col, 4) * 2 + lax.rem(col, 2))
        lines.append(side * 4 + lax.rem(tile_rows[s], 4))
    spot = jnp.zeros((1, 128), jnp.int32)
    line = jnp.zeros((1, 128), jnp.int32)
    for s in range(16):
        spot = jnp.where(slot == s, spots[s], spot)
        line = jnp.where(slot == s, lines[s], line)
    by_spot = jnp.where(part >= 4, lane - 64, spot)
    limit = jnp.where(part >= 4, 16, slot)
    found = jnp.full((1, 128), 16, jnp.int32)
    found_line, last_line = found, found
    for s in range(16):
        live = tile_count[0] > s
        found = jnp.where((by_spot == spots[s]) & (limit > s) & live, s, found)
        found_line = jnp.where((line == lines[s]) & (slot > s) & live, s, found_line)
        last_line = jnp.where((lane == lines[s]) & live, s, last_line)
    table = jnp.where(part == 0, spot, found)
    table = jnp.where(part == 1, found_line, table)
    table = jnp.where(part == 2, lax.rem(line, 4), table)
    return jnp.concatenate([table, last_line], axis=0)


def finish_kernel(*refs):
    sources, results, through, sems = refs[:4], refs[4:8], refs[8:12], refs[12]
    moves = [
        (
            pltpu.make_async_copy(sources[n], through[n], sems.at[n]),
            pltpu.make_async_copy(through[n], results[n], sems.at[n]),
        )
        for n in range(4)
    ]
    for read, _ in moves:
        read.start()
    for read, write in moves:
        read.wait()
        write.start()
    for _, write in moves:
        write.wait()


def per_device(features, weight, bias, tile_values, tile_rows, tile_cols, tile_count, cotangent):
    vmem, hbm = pltpu.VMEM, pl.BlockSpec(memory_space=pltpu.HBM)
    in_vmem = pl.BlockSpec(memory_space=pltpu.VMEM)
    square = (128, 128)
    shapes = (
        jax.ShapeDtypeStruct((512, 256), F32),
        jax.ShapeDtypeStruct((512, 128), F32),
        jax.ShapeDtypeStruct((128, 256), F32),
        jax.ShapeDtypeStruct((1, 256), F32),
    )
    outs = pl.pallas_call(
        kernel,
        out_shape=shapes,
        in_specs=[hbm] * 8,
        out_specs=(hbm, in_vmem, in_vmem, in_vmem),
        scratch_shapes=[
            pltpu.SMEM((16,), jnp.int32),
            pltpu.SMEM((16,), jnp.int32),
            pltpu.SMEM((1,), jnp.int32),
            vmem((2, 128), jnp.int32),
            vmem((2, 128), jnp.int32),
            pltpu.SMEM((2, 128), jnp.int32),
            pltpu.SMEM((2, 128), jnp.int32),
            vmem((64, 64, 128), F32),
            vmem((32, *square), F32),
            vmem((128, 256), F32),
            vmem((1, 256), F32),
            vmem((512, 256), F32),
            vmem((32, 128, 384), BF16),
            vmem((32, 128, 384), BF16),
            vmem((384, 256), BF16),
            vmem((768, 128), BF16),
            vmem((4, *square), F32),
            vmem((2, *square), F32),
            vmem((256, 128), F32),
            vmem((4, 64, 128), F32),
            vmem((64, 128), F32),
            vmem((64, 128), F32),
            vmem((8, 64, 128), F32),
            vmem((512, 256), F32),
            vmem((512, 256), F32),
            vmem((4, 384, 128), BF16),
            vmem((34, *square), F32),
            vmem((2, 4, 2, *square), F32),
            vmem((4, 2, *square), F32),
            vmem((2, 4, 2, *square), F32),
            vmem((4, 2, *square), F32),
            vmem((3, 4, 64, 128), F32),
            vmem((3, 4, 64, 128), F32),
            vmem((4, 4, 64, 128), F32),
            vmem((4, 3, 64, 128), F32),
            vmem((4, 64, 128), F32),
            vmem((3, 64, 128), F32),
            vmem((128, 256), F32),
            vmem((24, 256), F32),
            vmem((4, 24, 256), F32),
            vmem((24, 256), F32),
            vmem((4, 24, 256), F32),
            vmem((64, 128), F32),
            vmem((64, 128), F32),
            vmem((8, 64, 128), F32),
            vmem((8, 32, 128), F32),
            pltpu.SemaphoreType.DMA((12,)),
            pltpu.SemaphoreType.DMA((113,)),
            pltpu.SemaphoreType.DMA((113,)),
        ],
        compiler_params=pltpu.CompilerParams(
            collective_id=0, has_side_effects=True, vmem_limit_bytes=60 * 1024 * 1024
        ),
        cost_estimate=pl.CostEstimate(
            flops=400_000_000, bytes_accessed=4_000_000, transcendentals=131072
        ),
    )(
        tile_rows,
        tile_cols,
        tile_count,
        features.reshape(8, 64, 128),
        weight,
        bias[None, :],
        tile_values,
        cotangent,
    )
    output, grad_features, grad_weight, grad_bias = pl.pallas_call(
        finish_kernel,
        out_shape=shapes,
        in_specs=[hbm] * 4,
        out_specs=[hbm] * 4,
        scratch_shapes=[vmem(v.shape, F32) for v in shapes]
        + [pltpu.SemaphoreType.DMA((4,))],
    )(*outs)
    return output, grad_features, grad_weight, grad_bias[0]


def solution(mesh):
    return jax.shard_map(
        per_device,
        mesh=mesh,
        in_specs=(
            P("loop", None),
            P(),
            P(),
            P(("loop", "rep"), None, None),
            P(("loop", "rep")),
            P(("loop", "rep")),
            P(("loop", "rep")),
            P("loop", None),
        ),
        out_specs=(P("loop", None), P("loop", None), P(), P()),
        check_vma=False,
    )
```
